32 devices in a mesh: req: 2 (over x), hst: 16 (over z, y, core).
Axes of the slice: x: 2, y: 2, z: 4, core: 2. Of those that a mesh axis runs over, the one named last changes fastest.
Arguments:
- ctx_q: bfloat16 [4096, 4096], P(('req', 'hst')), parts along dimension 0, may hold values from -24 to 24
- ctx_k: bfloat16 [4096, 512], P(('req', 'hst')), parts along dimension 0, may hold values from -8 to 8
- ctx_v: bfloat16 [4096, 512], P(('req', 'hst')), parts along dimension 0, may hold values from -6 to 6
- ask_q: bfloat16 [64, 4096], P(('req', 'hst')), parts along dimension 0, may hold values from -24 to 24
- ask_k: bfloat16 [64, 512], P(('req', 'hst')), parts along dimension 0, may hold values from -9 to 9
- ask_v: bfloat16 [64, 512], P(('req', 'hst')), parts along dimension 0, may hold values from -6 to 6
- valid: int32 [32], P(('req', 'hst')), parts along dimension 0, may hold values from 64 to 128, as said below
Outputs:
- ctx_out: bfloat16 [4096, 4096], P(('req', 'hst')), parts along dimension 0
- ask_out: bfloat16 [64, 4096], P(('req', 'hst')), parts along dimension 0
The draws below stay inside these ranges and needn't reach their ends.
There are 2 independent parts, one for each index of `req`. The reference program is written for one: setup_inputs(seed, part) draws one part's arguments, and reference() takes and returns one part's arrays. A program takes and returns all parts, laid end to end along the dimension named above; each array names one. Nothing has to cross between parts.
Inputs may be any that keep to these rules, and one draw needn't show every extreme that they name: `valid`: block 0, the anchor, is always full.
All inputs are finite; a program needn't handle non-finite values.
Results may differ from the reference program's by a relative error of at most 0.0029.
Values may be sent and summed in bfloat16 or wider, within the bound.
A program may use at most 320 MiB of HBM per device.

```python
import math
import jax
import jax.numpy as jnp
from jax import lax

H = 32
KVH = 4
DH = 128
BLOCK = 128
TOKENS = 2048
QLEN = 32
N_HST = 16


def draw_ctx_q(key, part):
    values = jnp.clip(jax.random.normal(jax.random.fold_in(key, 1), (TOKENS, H * DH)) * 2.5, -10.0, 10.0)
    return values.astype(jnp.bfloat16)


def draw_ctx_k(key, part):
    values = jnp.clip(jax.random.normal(jax.random.fold_in(key, 5), (TOKENS, KVH * DH)), -6.0, 6.0)
    return values.astype(jnp.bfloat16)


def draw_ask_q(key, part):
    values = jnp.clip(jax.random.normal(jax.random.fold_in(key, 11), (QLEN, H * DH)) * 2.5, -10.0, 10.0)
    return values.astype(jnp.bfloat16)


def draw_valid(key, part):
    host_count = TOKENS // BLOCK
    counts = jax.random.randint(jax.random.fold_in(key, 21), (host_count,), BLOCK // 2, BLOCK + 1)
    lowest = jax.random.randint(jax.random.fold_in(key, 22), (), 1, host_count)
    counts = counts.at[lowest].set(BLOCK // 2)
    counts = counts.at[0].set(BLOCK)
    return counts.astype(jnp.int32)


def block_scale(key, dims, cuts, smallest, high):
    loudness = 1.0
    for axis_at, parts in cuts:
        steps = jax.random.uniform(jax.random.fold_in(jax.random.fold_in(key, 6), axis_at), (parts,), jnp.float32, smallest / len(cuts), high / len(cuts))
        loudness = loudness * jnp.repeat(jnp.exp(steps), dims[axis_at] // parts).reshape((-1,) + (1,) * (len(dims) - 1 - axis_at))
    return loudness


def normal_values(stream_key, shape, spread, limit, cuts=(), held_as=jnp.bfloat16):
    loudness = block_scale(stream_key, shape, cuts, -0.22, 0.18) if cuts else 1.0
    result = jax.random.normal(stream_key, shape, jnp.float32) * spread * loudness
    return jnp.minimum(jnp.maximum(result, -limit), limit).astype(held_as)


def setup_inputs(seed: int = 0, part: int = 0) -> dict:
    seeds = jax.random.split(jax.random.key(seed), 8)
    part_splits = jax.random.split(jax.random.fold_in(seeds[7], part), 8)
    ctx_q = draw_ctx_q(jax.random.fold_in(jax.random.fold_in(seeds[7], part), 71), part)
    ctx_k = draw_ctx_k(jax.random.fold_in(jax.random.fold_in(seeds[7], part), 71), part)
    ctx_v = normal_values(part_splits[2], (TOKENS, KVH * DH), 1.0, 6.0, ((0, 16),))
    ask_q = draw_ask_q(jax.random.fold_in(jax.random.fold_in(seeds[7], part), 71), part)
    ask_k = normal_values(part_splits[4], (QLEN, KVH * DH), 1.5, 9.0, ((0, 16),))
    ask_v = normal_values(part_splits[5], (QLEN, KVH * DH), 1.0, 6.0, ((0, 16),))
    valid = draw_valid(jax.random.fold_in(jax.random.fold_in(seeds[7], part), 71), part)
    return dict(ctx_q=ctx_q, ctx_k=ctx_k, ctx_v=ctx_v, ask_q=ask_q, ask_k=ask_k, ask_v=ask_v, valid=valid)


def partial_attend(queries, key_rows, value_rows, visible):
    row_count = queries.shape[0]
    span_count = key_rows.shape[0]
    group_size = H // KVH
    query_f = queries.astype(jnp.float32).reshape(row_count, KVH, group_size, DH)
    key_f = key_rows.astype(jnp.float32).reshape(span_count, KVH, DH)
    value_f = value_rows.astype(jnp.float32).reshape(span_count, KVH, DH)
    scores = jnp.einsum('rkgd,skd->rkgs', query_f, key_f) * (1.0 / math.sqrt(DH))
    scores = jnp.where(visible[:, None, None, :], scores, -jnp.inf)
    row_max = lax.optimization_barrier(jnp.max(scores, axis=-1))
    expon = jnp.exp(scores - row_max[..., None])
    row_sum = lax.optimization_barrier(jnp.sum(expon, axis=-1))
    rounded = lax.optimization_barrier(expon.astype(jnp.bfloat16)).astype(jnp.float32)
    mixed = jnp.einsum('rkgs,skd->rkgd', rounded, value_f)
    return (row_max.reshape(row_count, H), row_sum.reshape(row_count, H), mixed.reshape(row_count, H * DH))

def weigh(values, factor):
    shape = values.shape
    return (values.reshape(shape[:-1] + (H, DH)) * factor[..., None]).reshape(shape)

def reference(ctx_q, ctx_k, ctx_v, ask_q, ask_k, ask_v, valid):
    local = jnp.arange(BLOCK, dtype=jnp.int32)
    anchor_k = ctx_k[:BLOCK]
    anchor_v = ctx_v[:BLOCK]

    def context_block(block_index):
        start = (block_index * BLOCK).astype(jnp.int32)
        queries = lax.dynamic_slice_in_dim(ctx_q, start, BLOCK, 0)
        own_k = lax.dynamic_slice_in_dim(ctx_k, start, BLOCK, 0)
        own_v = lax.dynamic_slice_in_dim(ctx_v, start, BLOCK, 0)
        valid_count = valid[block_index]
        own_visible = (local[None, :] <= local[:, None]) & (local[None, :] < valid_count)
        anchor_visible = jnp.broadcast_to(block_index > 0, (BLOCK, BLOCK))
        visible = jnp.concatenate([anchor_visible, own_visible], axis=1)
        row_max, row_sum, mixed = partial_attend(queries, jnp.concatenate([anchor_k, own_k], 0), jnp.concatenate([anchor_v, own_v], 0), visible)
        normed = weigh(mixed, 1.0 / row_sum)
        return jnp.where(local[:, None] < valid_count, normed, 0.0).astype(jnp.bfloat16)
    ctx_out = lax.map(context_block, jnp.arange(N_HST, dtype=jnp.int32)).reshape(TOKENS, H * DH)
    query_pos = jnp.arange(QLEN, dtype=jnp.int32)
    causal = query_pos[None, :] <= query_pos[:, None]

    def host_step(carry, block_index):
        best, total, summed = carry
        start = (block_index * BLOCK).astype(jnp.int32)
        own_k = lax.dynamic_slice_in_dim(ctx_k, start, BLOCK, 0)
        own_v = lax.dynamic_slice_in_dim(ctx_v, start, BLOCK, 0)
        valid_count = valid[block_index]
        visible = jnp.concatenate([jnp.broadcast_to(local[None, :] < valid_count, (QLEN, BLOCK)), causal & (block_index == N_HST - 1)], axis=1)
        row_max, row_sum, mixed = partial_attend(ask_q, jnp.concatenate([own_k, ask_k], 0), jnp.concatenate([own_v, ask_v], 0), visible)
        new_best = jnp.maximum(best, row_max)
        old_weight = jnp.exp(best - new_best)
        new_weight = jnp.exp(row_max - new_best)
        return ((new_best, total * old_weight + row_sum * new_weight, weigh(summed, old_weight) + weigh(mixed, new_weight)), None)
    start_carry = (jnp.full((QLEN, H), -jnp.inf, jnp.float32), jnp.zeros((QLEN, H), jnp.float32), jnp.zeros((QLEN, H * DH), jnp.float32))
    (best, total, summed), _ = lax.scan(host_step, start_carry, jnp.arange(N_HST, dtype=jnp.int32))
    ask_out = weigh(summed, 1.0 / total).astype(jnp.bfloat16)
    return (ctx_out, ask_out)
```

```python
import functools
import math

import jax
import jax.numpy as jnp
from jax import lax
from jax.experimental import pallas as pl
from jax.experimental.pallas import tpu as pltpu
from jax.sharding import PartitionSpec as P

KVH = 4
DH = 128
PAIR = 2
TAIL = 8
C = math.log2(math.e) / math.sqrt(DH)
NT = (((1,), (1,)), ((), ()))
NN = (((1,), (0,)), ((), ()))


def remote(src, dst, send_sem, recv_sem, target):
    return pltpu.make_async_remote_copy(
        src_ref=src,
        dst_ref=dst,
        send_sem=send_sem,
        recv_sem=recv_sem,
        device_id={"hst": target},
        device_id_type=pl.DeviceIdType.MESH,
    )


def kernel(
    n, ctx_q, ctx_k, ctx_v, ask_q, ask_k, ask_v, valid, obuf, numr,
    qbuf, kc, kvall, cnt, qraw, kraw, vraw, stage, pack, qall, selfkv, num,
    s_kv, s_an, s_q, s_own, s_raw,
    q_s, q_r, k_s, k_r, c_s, c_r, a_s, a_r, f_s, r_s, n_s, n_r,
):
    rows = ctx_q.shape[0]
    G = ctx_q.shape[1] // (KVH * DH)
    tokens = ask_q.shape[0]
    tile = pack.shape[2]
    planes = n // KVH
    span = KVH * tile
    me = lax.axis_index("hst")
    p = me // KVH
    m = me % KVH
    is_root = me == 0
    is_last = p == planes - 1
    far = (m + 2) % KVH
    even = m % 2 == 0
    hub = (p == 0) & (m == 2)
    near = p == 1

    barrier = pltpu.get_barrier_semaphore()

    @pl.loop(1, n)
    def _(d):
        pl.semaphore_signal(
            barrier, inc=1, device_id={"hst": (me + d) % n}, device_id_type=pl.DeviceIdType.MESH
        )

    def cols(g):
        return pl.ds(pl.multiple_of(g * DH, DH), DH)

    def wide(g):
        return pl.ds(pl.multiple_of(g * (G * DH), G * DH), G * DH)

    raw_loads = [
        pltpu.make_async_copy(ask_q, qraw, s_raw.at[0]),
        pltpu.make_async_copy(ask_k, kraw, s_raw.at[1]),
        pltpu.make_async_copy(ask_v, vraw, s_raw.at[2]),
    ]
    for copy in raw_loads:
        copy.start()

    def load_kv(g, i, half, sem):
        src = (ctx_k, ctx_v)[i]
        return pltpu.make_async_copy(src.at[:, cols(g)], kc.at[g, i, half], sem.at[g, i])

    for g in range(KVH):
        for i in range(2):
            load_kv(g, i, 1, s_kv).start()

    @pl.when(is_root)
    def _():
        for g in range(KVH):
            for i in range(2):
                load_kv(g, i, 0, s_an).start()

    def q_load(g):
        return pltpu.make_async_copy(ctx_q.at[:, wide(g)], qbuf.at[:, wide(g)], s_q.at[g])

    for g in range(KVH):
        q_load(g).start()

    own_kv = [
        pltpu.make_async_copy(ctx_k.at[:, cols(m)], kvall.at[m, 0], s_own.at[0]),
        pltpu.make_async_copy(ctx_v.at[:, cols(m)], kvall.at[m, 1], s_own.at[1]),
    ]
    for copy in own_kv:
        copy.start()

    for copy in raw_loads:
        copy.wait()
    for g in range(KVH):
        for h in range(G):
            at = (g * G + h) * DH
            stage[g, 0, pl.ds(h * tokens, tokens), :] = qraw[:, at : at + DH].astype(jnp.float32)
        for i, raw in ((1, kraw), (2, vraw)):
            stage[g, i] = jnp.zeros((tile, DH), jnp.float32)
            stage[g, i, pl.ds(0, tokens), :] = raw[:, g * DH : g * DH + DH].astype(jnp.float32)
    pack[...] = stage[...].astype(jnp.bfloat16)
    cnt[m] = jnp.full((tile, DH), valid[0].astype(jnp.float32)).astype(jnp.bfloat16)
    qall[me] = pack[m, 0]

    @pl.when(is_last)
    def _():
        selfkv[me] = pack[m, pl.ds(1, 2)]

    for g in range(KVH):
        for i in range(2):
            load_kv(g, i, 1, s_kv).wait()

    def context(g):
        q_load(g).wait()
        count = cnt[m].astype(jnp.float32)[0:1, :]
        row = lax.broadcasted_iota(jnp.int32, (rows, rows), 0)
        lane = lax.broadcasted_iota(jnp.int32, (rows, rows), 1)
        own = (lane <= row) & (lane.astype(jnp.float32) < count)
        outer = jnp.broadcast_to(me, (rows, rows)) > 0
        visible = jnp.concatenate([outer, own], axis=1)
        kept = lax.broadcasted_iota(jnp.int32, (rows, DH), 0).astype(jnp.float32) < count
        keys = kc[g, 0].reshape(2 * rows, DH)
        values = kc[g, 1].reshape(2 * rows, DH)
        at = [pl.ds(pl.multiple_of((g * G + k) * DH, DH), DH) for k in range(G)]
        s = [
            lax.dot_general(qbuf[:, x], keys, NT, preferred_element_type=jnp.float32)
            for x in at
        ]
        s = [jnp.where(visible, x, -jnp.inf) for x in s]
        top = [jnp.max(x, axis=1, keepdims=True) for x in s]
        e = [jnp.exp2((x - y) * C) for x, y in zip(s, top)]
        total = [jnp.sum(x, axis=1, keepdims=True) for x in e]
        mixed = [
            lax.dot_general(x.astype(jnp.bfloat16), values, NN, preferred_element_type=jnp.float32)
            for x in e
        ]
        for k in range(G):
            out = jnp.where(kept, mixed[k] * (1.0 / total[k]), 0.0)
            obuf[:, at[k]] = out.astype(jnp.bfloat16)

    @pl.when(is_root)
    def _():
        for g in range(KVH):
            for i in range(2):
                load_kv(g, i, 0, s_an).wait()

        @pl.loop(0, KVH)
        def _(g):
            context(g)

    pl.semaphore_wait(barrier, n - 1)

    def q_send(d):
        target = (me + n - d) % n
        return remote(pack.at[target % KVH, 0], qall.at[me], q_s.at[d], q_r.at[me], target)

    @pl.loop(1, n)
    def _(d):
        q_send(d).start()

    def self_send(g):
        return remote(
            pack.at[g, pl.ds(1, 2)], selfkv.at[me], f_s.at[g], r_s.at[me], n - KVH + g
        )

    for g in range(KVH):
        @pl.when(me != n - KVH + g)
        def _():
            self_send(g).start()

    def chunk_send(g, slot, target):
        piece = kc.at[g, :, 0]
        return remote(piece, piece, a_s.at[g, slot], a_r.at[g], target)

    def across(g):
        return chunk_send(g, 0, p * KVH + far)

    def beside(g):
        return chunk_send(g, 1, p * KVH + m + 1)

    def along(g, q):
        return chunk_send(g, 1 + q, q * KVH + m)

    def cnt_send(d):
        g = (m + d) % KVH
        return remote(cnt.at[m], cnt.at[m], c_s.at[d], c_r.at[m], p * KVH + g)

    def kv_send(d):
        g = (m + d) % KVH
        return remote(kc.at[g, :, 1], kvall.at[m], k_s.at[d], k_r.at[m], p * KVH + g)

    @pl.when(is_root)
    def _():
        for g in (2, 3):
            across(g).start()
        for g in range(KVH):
            along(g, 1).start()

    for d in (2, 3, 1):
        kv_send(d).start()
        cnt_send(d).start()

    @pl.when(is_root)
    def _():
        for g in range(KVH):
            beside(g).start()
        for q in range(2, planes):
            for g in (0, 1):
                along(g, q).start()
        for g in (0, 1):
            across(g).start()

    first = jnp.where(near, 0, m // 2 * 2)
    second = 2 - first

    def chunk_wait(g):
        chunk_send(g, 0, me).wait_recv()

    def take_first():
        @pl.when(jnp.logical_not(is_root))
        def _():
            for k in range(2):
                g = first + k
                chunk_wait(g)

                @pl.when(hub)
                def _():
                    for q in range(2, planes):
                        along(g, q).start()

                @pl.when((near & (m == 0)) | (even & (p > 1)))
                def _():
                    across(g).start()

                @pl.when(even)
                def _():
                    beside(g).start()

    def take_second():
        @pl.when(jnp.logical_not(is_root))
        def _():
            for k in range(2):
                g = second + k
                chunk_wait(g)

                @pl.when(near & (m == 0))
                def _():
                    across(g).start()

                @pl.when(even)
                def _():
                    beside(g).start()

    early = hub | (near & (m == 0))

    @pl.when(early)
    def _():
        take_first()

    for copy in own_kv:
        copy.wait()
    for d in range(1, KVH):
        j = (m + d) % KVH
        remote(cnt.at[0], cnt.at[j], c_s.at[0], c_r.at[j], me).wait_recv()
        remote(kc.at[0, :, 1], kvall.at[j], k_s.at[0], k_r.at[j], me).wait_recv()

    def num_send(owner):
        return remote(num.at[owner], numr.at[me], n_s.at[owner], n_r.at[me], owner)

    def q_wait(q):
        for j in range(KVH):
            source = q * KVH + j

            @pl.when(source != me)
            def _():
                remote(
                    pack.at[0, 0], qall.at[source], q_s.at[0], q_r.at[source], me
                ).wait_recv()

    diag = lax.broadcasted_iota(jnp.int32, (span, DH), 0) == lax.broadcasted_iota(
        jnp.int32, (span, DH), 1
    )

    def ask(with_self):
        total_rows = PAIR * span
        lane = lax.broadcasted_iota(jnp.int32, (total_rows, rows), 1).astype(jnp.float32)

        @pl.loop(0, planes // PAIR)
        def _(step):
            at_planes = [step * PAIR + k for k in range(PAIR)]
            for q in at_planes:
                q_wait(q)
            queries = jnp.concatenate(
                [qall[pl.ds(q * KVH, KVH)].reshape(span, DH) for q in at_planes], axis=0
            )
            s = [
                lax.dot_general(queries, kvall[j, 0], NT, preferred_element_type=jnp.float32)
                for j in range(KVH)
            ]
            s = [
                jnp.where(lane < cnt[j].astype(jnp.float32)[0:1, :], s[j], -jnp.inf)
                for j in range(KVH)
            ]
            values = [kvall[j, 1] for j in range(KVH)]
            top = [jnp.max(x, axis=1, keepdims=True) for x in s]
            if with_self:
                keys = selfkv[:, 0].reshape(n * tile, DH)
                s2 = lax.dot_general(queries, keys, NT, preferred_element_type=jnp.float32)
                shape = (total_rows, n * tile)
                at = lax.broadcasted_iota(jnp.int32, shape, 1)
                row = lax.broadcasted_iota(jnp.int32, shape, 0)
                shift = tile.bit_length() - 1
                u = (at >> shift) * tokens + (at & (tile - 1))
                t = ((at_planes[0] * span + row) >> shift) * tokens + (row & (tokens - 1))
                s2 = jnp.where(((at & (tile - 1)) < tokens) & (u <= t), s2, -jnp.inf)
                s[-1] = jnp.concatenate([s[-1], s2], axis=1)
                values[-1] = jnp.concatenate(
                    [values[-1], selfkv[:, 1].reshape(n * tile, DH)], axis=0
                )
                top[-1] = jnp.maximum(top[-1], jnp.max(s2, axis=1, keepdims=True))
            e = [jnp.exp2((x - y) * C) for x, y in zip(s, top)]
            part = [jnp.sum(x, axis=1, keepdims=True) for x in e]
            mixed = [
                lax.dot_general(
                    x.astype(jnp.bfloat16), v, NN, preferred_element_type=jnp.float32
                )
                for x, v in zip(e, values)
            ]
            best = functools.reduce(jnp.maximum, top)
            factor = [jnp.exp2((x - best) * C) for x in top]
            total = sum(x * y for x, y in zip(part, factor))
            summed = sum(x * y for x, y in zip(mixed, factor))
            pick = lax.broadcasted_iota(jnp.int32, (TAIL, DH), 0) == 0
            for k, q in enumerate(at_planes):
                cut = slice(k * span, (k + 1) * span)
                line1 = jnp.sum(jnp.where(diag, best[cut], 0.0), axis=0, keepdims=True)
                line2 = jnp.sum(jnp.where(diag, total[cut], 0.0), axis=0, keepdims=True)
                tail = jnp.where(pick, line1, line2)
                for j in range(KVH):
                    owner = q * KVH + j
                    at = k * span + j * tile
                    num[owner, pl.ds(0, tile)] = summed[at : at + tile]
                    num[owner, pl.ds(tile, TAIL)] = tail

                    @pl.when(owner != me)
                    def _():
                        num_send(owner).start()

    @pl.when(is_last)
    def _():
        @pl.loop(1, n)
        def _(d):
            source = (me + d) % n
            remote(
                pack.at[0, pl.ds(1, 2)], selfkv.at[source], f_s.at[0], r_s.at[source], me
            ).wait_recv()

        ask(True)

    @pl.when(jnp.logical_not(is_last))
    def _():
        ask(False)

    numr[me] = num[me]

    @pl.when(jnp.logical_not(early))
    def _():
        take_first()

    @pl.when(jnp.logical_not(is_root))
    def _():
        @pl.loop(0, 2)
        def _(k):
            context(first + k)

    take_second()

    @pl.when(jnp.logical_not(is_root))
    def _():
        @pl.loop(0, 2)
        def _(k):
            context(second + k)

    @pl.loop(1, n)
    def _(d):
        q_send(d).wait_send()
        source = (me + d) % n
        num_send(source).wait_send()
        remote(num.at[0], numr.at[source], n_s.at[0], n_r.at[source], me).wait_recv()

    for d in range(1, KVH):
        cnt_send(d).wait_send()
        kv_send(d).wait_send()
    for g in range(KVH):
        @pl.when(me != n - KVH + g)
        def _():
            self_send(g).wait_send()

    @pl.when(is_root)
    def _():
        for g in range(KVH):
            across(g).wait_send()
            along(g, 1).wait_send()
        for q in range(2, planes):
            for g in (0, 1):
                along(g, q).wait_send()

    @pl.when(even)
    def _():
        for g in range(KVH):
            beside(g).wait_send()

    @pl.when(near & (m == 0))
    def _():
        for g in range(KVH):
            across(g).wait_send()

    @pl.when(even & (p > 1))
    def _():
        for k in range(2):
            across(first + k).wait_send()

    @pl.when(hub)
    def _():
        for k in range(2):
            for q in range(2, planes):
                along(first + k, q).wait_send()


def finish(obuf, numr, ctx_out, ask_out, fin, aout, s_out):
    n, size, _ = numr.shape
    tile = size - TAIL
    tokens = ask_out.shape[0]
    G = tile // tokens
    planes = n // KVH
    span = KVH * tile
    m = lax.axis_index("hst") % KVH
    ctx_copy = pltpu.make_async_copy(obuf, ctx_out, s_out.at[0])
    ctx_copy.start()
    row = lax.broadcasted_iota(jnp.int32, (span, DH), 0)
    lane = lax.broadcasted_iota(jnp.int32, (span, DH), 1)
    diag = lane == (row & (tile - 1)) + m * tile

    def column(line):
        line = jnp.broadcast_to(line, (KVH, tile, DH)).reshape(span, DH)
        return jnp.sum(jnp.where(diag, line, 0.0), axis=1, keepdims=True)

    top, part, mixed = [], [], []
    for q in range(planes):
        at = pl.ds(q * KVH, KVH)
        top.append(column(numr[at, pl.ds(tile, 1)]))
        part.append(column(numr[at, pl.ds(tile + 1, 1)]))
        mixed.append(numr[at, pl.ds(0, tile)].reshape(span, DH))
    best = functools.reduce(jnp.maximum, top)
    factor = [jnp.exp2((x - best) * C) for x in top]
    total = sum(x * y for x, y in zip(part, factor))
    summed = sum(x * y for x, y in zip(mixed, factor))
    fin[...] = summed * (1.0 / total)
    for g in range(KVH):
        for h in range(G):
            at = (g * G + h) * DH
            aout[:, at : at + DH] = fin[pl.ds(g * tile + h * tokens, tokens), :].astype(jnp.bfloat16)
    ask_copy = pltpu.make_async_copy(aout, ask_out, s_out.at[1])
    ask_copy.start()
    ask_copy.wait()
    ctx_copy.wait()


def body(n, ctx_q, ctx_k, ctx_v, ask_q, ask_k, ask_v, valid):
    rows, width = ctx_q.shape
    tokens = ask_q.shape[0]
    G = width // (KVH * DH)
    tile = tokens * G
    planes = n // KVH
    dma = pltpu.SemaphoreType.DMA
    bf = jnp.bfloat16
    f32 = jnp.float32
    large = [
        pltpu.with_memory_space_constraint(x, pltpu.HBM)
        for x in (ctx_q, ctx_k, ctx_v, ask_q, ask_k, ask_v)
    ]
    hbm = pl.BlockSpec(memory_space=pltpu.HBM)
    vmem = pl.BlockSpec(memory_space=pltpu.VMEM)
    obuf, numr = pl.pallas_call(
        functools.partial(kernel, n),
        out_shape=(
            jax.ShapeDtypeStruct(ctx_q.shape, bf),
            jax.ShapeDtypeStruct((n, tile + TAIL, DH), f32),
        ),
        in_specs=[hbm] * 6 + [pl.BlockSpec(memory_space=pltpu.SMEM)],
        out_specs=(vmem, vmem),
        scratch_shapes=[
            pltpu.VMEM(ctx_q.shape, bf),
            pltpu.VMEM((KVH, 2, 2, rows, DH), bf),
            pltpu.VMEM((KVH, 2, rows, DH), bf),
            pltpu.VMEM((KVH, tile, DH), bf),
            pltpu.VMEM(ask_q.shape, bf),
            pltpu.VMEM(ask_k.shape, bf),
            pltpu.VMEM(ask_v.shape, bf),
            pltpu.VMEM((KVH, 3, tile, DH), f32),
            pltpu.VMEM((KVH, 3, tile, DH), bf),
            pltpu.VMEM((n, tile, DH), bf),
            pltpu.VMEM((n, 2, tile, DH), bf),
            pltpu.VMEM((n, tile + TAIL, DH), f32),
            dma((KVH, 2)),
            dma((KVH, 2)),
            dma((KVH,)),
            dma((2,)),
            dma((3,)),
            dma((n,)),
            dma((n,)),
            dma((KVH,)),
            dma((KVH,)),
            dma((KVH,)),
            dma((KVH,)),
            dma((KVH, planes + 1)),
            dma((KVH,)),
            dma((KVH,)),
            dma((n,)),
            dma((n,)),
            dma((n,)),
        ],
        compiler_params=pltpu.CompilerParams(
            collective_id=0, has_side_effects=True, vmem_limit_bytes=16 << 20
        ),
    )(*large, valid)
    return pl.pallas_call(
        finish,
        out_shape=(
            jax.ShapeDtypeStruct(ctx_q.shape, bf),
            jax.ShapeDtypeStruct(ask_q.shape, bf),
        ),
        in_specs=[vmem, vmem],
        out_specs=(hbm, hbm),
        scratch_shapes=[
            pltpu.VMEM((KVH * tile, DH), f32),
            pltpu.VMEM(ask_q.shape, bf),
            dma((2,)),
        ],
        compiler_params=pltpu.CompilerParams(vmem_limit_bytes=8 << 20),
    )(obuf, numr)


def solution(mesh):
    n = mesh.shape["hst"]
    rows = P(("req", "hst"), None)
    return jax.shard_map(
        functools.partial(body, n),
        mesh=mesh,
        in_specs=(rows,) * 6 + (P(("req", "hst")),),
        out_specs=(rows, rows),
        check_vma=False,
    )
```

```python
import functools
import math

import jax
import jax.numpy as jnp
from jax import lax
from jax.experimental import pallas as pl
from jax.experimental.pallas import tpu as pltpu
from jax.sharding import PartitionSpec as P

KVH = 4
DH = 128
PAIR = 2
TAIL = 8
C = math.log2(math.e) / math.sqrt(DH)
NT = (((1,), (1,)), ((), ()))
NN = (((1,), (0,)), ((), ()))


def remote(src, dst, send_sem, recv_sem, target):
    return pltpu.make_async_remote_copy(
        src_ref=src,
        dst_ref=dst,
        send_sem=send_sem,
        recv_sem=recv_sem,
        device_id={"hst": target},
        device_id_type=pl.DeviceIdType.MESH,
    )


def kernel(
    n, ctx_q, ctx_k, ctx_v, ask_q, ask_k, ask_v, valid, obuf, numr,
    qbuf, kc, kvall, cnt, qraw, kraw, vraw, stage, pack, qall, selfkv, num, count_ref,
    s_kv, s_an, s_q, s_own, s_raw,
    q_s, q_r, k_s, k_r, c_s, c_r, across_s, beside_s, near_s, far_s, a_r, f_s, r_s, n_s, n_r, go,
):
    rows = ctx_q.shape[0]
    G = ctx_q.shape[1] // (KVH * DH)
    tokens = ask_q.shape[0]
    tile = pack.shape[2]
    planes = n // KVH
    span = KVH * tile
    me = lax.axis_index("hst")
    p = me // KVH
    m = me % KVH
    is_root = me == 0
    is_last = p == planes - 1
    far = (m + 2) % KVH
    even = m % 2 == 0
    hub = (p == 0) & (m == 2)
    near = p == 1

    barrier = pltpu.get_barrier_semaphore()

    child = (me == 1) | (me == 2) | (me == KVH)

    def signal(sem, target):
        pl.semaphore_signal(
            sem, inc=1, device_id={"hst": target}, device_id_type=pl.DeviceIdType.MESH
        )

    @pl.when(child)
    def _():
        signal(barrier, 0)

    @pl.loop(1, n)
    def _(d):
        target = (me + d) % n

        @pl.when(target != 0)
        def _():
            signal(barrier, target)

    def drain(ref, sem):
        pltpu.make_async_copy(ref, ref, sem).wait()

    def cols(g):
        return pl.ds(pl.multiple_of(g * DH, DH), DH)

    raw_loads = [
        pltpu.make_async_copy(ask_q, qraw, s_raw.at[0]),
        pltpu.make_async_copy(ask_k, kraw, s_raw.at[1]),
        pltpu.make_async_copy(ask_v, vraw, s_raw.at[2]),
        pltpu.make_async_copy(valid, count_ref, s_raw.at[3]),
    ]
    for copy in raw_loads:
        copy.start()

    def load_kv(g, i, half, sem):
        src = (ctx_k, ctx_v)[i]
        return pltpu.make_async_copy(src.at[:, cols(g)], kc.at[g, i, half], sem)

    for g in range(KVH):
        for i in range(2):
            load_kv(g, i, 1, s_kv).start()

    @pl.when(is_root)
    def _():
        for g in range(KVH):
            for i in range(2):
                load_kv(g, i, 0, s_an).start()

    q_load = pltpu.make_async_copy(ctx_q, qbuf, s_q)
    q_load.start()

    own_kv = [
        pltpu.make_async_copy(ctx_k.at[:, cols(m)], kvall.at[m, 0], s_own),
        pltpu.make_async_copy(ctx_v.at[:, cols(m)], kvall.at[m, 1], s_own),
    ]
    for copy in own_kv:
        copy.start()

    for copy in raw_loads:
        copy.wait()
    for g in range(KVH):
        for h in range(G):
            at = (g * G + h) * DH
            stage[g, 0, pl.ds(h * tokens, tokens), :] = qraw[:, at : at + DH].astype(jnp.float32)
        for i, raw in ((1, kraw), (2, vraw)):
            stage[g, i] = jnp.zeros((tile, DH), jnp.float32)
            stage[g, i, pl.ds(0, tokens), :] = raw[:, g * DH : g * DH + DH].astype(jnp.float32)
    pack[...] = stage[...].astype(jnp.bfloat16)
    cnt[m] = jnp.full((tile, DH), count_ref[0].astype(jnp.float32)).astype(jnp.bfloat16)
    qall[me] = pack[m, 0]

    @pl.when(is_last)
    def _():
        selfkv[me] = pack[m, pl.ds(1, 2)]

    drain(kc.at[:, :, 1], s_kv)
    drain(kvall.at[m], s_own)
    q_load.wait()

    def context(g):
        count = cnt[m].astype(jnp.float32)[0:1, :]
        row = lax.broadcasted_iota(jnp.int32, (rows, rows), 0)
        lane = lax.broadcasted_iota(jnp.int32, (rows, rows), 1)
        own = (lane <= row) & (lane.astype(jnp.float32) < count)
        outer = jnp.broadcast_to(me, (rows, rows)) > 0
        visible = jnp.concatenate([outer, own], axis=1)
        kept = lax.broadcasted_iota(jnp.int32, (rows, DH), 0).astype(jnp.float32) < count
        keys = kc[g, 0].reshape(2 * rows, DH)
        values = kc[g, 1].reshape(2 * rows, DH)
        at = [pl.ds(pl.multiple_of((g * G + k) * DH, DH), DH) for k in range(G)]
        s = [
            lax.dot_general(qbuf[:, x], keys, NT, preferred_element_type=jnp.float32)
            for x in at
        ]
        s = [jnp.where(visible, x, -jnp.inf) for x in s]
        top = [jnp.max(x, axis=1, keepdims=True) for x in s]
        e = [jnp.exp2((x - y) * C) for x, y in zip(s, top)]
        total = [jnp.sum(x, axis=1, keepdims=True) for x in e]
        mixed = [
            lax.dot_general(x.astype(jnp.bfloat16), values, NN, preferred_element_type=jnp.float32)
            for x in e
        ]
        for k in range(G):
            out = jnp.where(kept, mixed[k] * (1.0 / total[k]), 0.0)
            obuf[:, at[k]] = out.astype(jnp.bfloat16)

    def chunk_send(g, sem, target):
        piece = kc.at[g, :, 0]
        return remote(piece, piece, sem, a_r.at[g], target)

    def across(g):
        return chunk_send(g, across_s, p * KVH + far)

    def beside(g):
        return chunk_send(g, beside_s, p * KVH + m + 1)

    def along_near(g):
        return chunk_send(g, near_s, KVH)

    def along_far(g, k, q):
        return chunk_send(g, far_s.at[k], q * KVH + m)

    @pl.when(is_root)
    def _():
        drain(kc.at[:, :, 0], s_an)

        @pl.loop(0, 2)
        def _(g):
            context(g)

        pl.semaphore_wait(barrier, 3)
        for g in (2, 3):
            across(g).start()
        for g in range(KVH):
            along_near(g).start()
        for g in range(KVH):
            beside(g).start()
        for g in (0, 1):
            across(g).start()

        @pl.loop(2, KVH)
        def _(g):
            context(g)

        pl.semaphore_wait(go, 1)

    @pl.when(jnp.logical_not(is_root))
    def _():
        pl.semaphore_wait(barrier, n - 1)

    @pl.when(me == 1)
    def _():
        signal(go, 0)

    def q_send(d):
        target = (me + n - d) % n
        return remote(pack.at[target % KVH, 0], qall.at[me], q_s, q_r.at[p], target)

    @pl.loop(1, n)
    def _(d):
        q_send(d).start()

    def self_send(g):
        return remote(pack.at[g, pl.ds(1, 2)], selfkv.at[me], f_s, r_s, n - KVH + g)

    for g in range(KVH):
        @pl.when(me != n - KVH + g)
        def _():
            self_send(g).start()

    def cnt_send(d):
        g = (m + d) % KVH
        return remote(cnt.at[m], cnt.at[m], c_s, c_r, p * KVH + g)

    def kv_send(d):
        g = (m + d) % KVH
        return remote(kc.at[g, :, 1], kvall.at[m], k_s, k_r, p * KVH + g)

    for d in (2, 3, 1):
        kv_send(d).start()
        cnt_send(d).start()

    @pl.when(is_root)
    def _():
        for q in range(planes - 1, 1, -1):
            for g in (0, 1):
                along_far(g, g, q).start()

    first = jnp.where(near, 0, m // 2 * 2)
    second = 2 - first

    def chunk_wait(g):
        drain(kc.at[g, :, 0], a_r.at[g])

    def take_first():
        @pl.when(jnp.logical_not(is_root))
        def _():
            for k in range(2):
                g = first + k
                chunk_wait(g)

                @pl.when(hub)
                def _():
                    for q in range(planes - 1, 1, -1):
                        along_far(g, k, q).start()

                @pl.when((near & (m == 0)) | (even & (p > 1)))
                def _():
                    across(g).start()

                @pl.when(even)
                def _():
                    beside(g).start()

    def take_second():
        @pl.when(jnp.logical_not(is_root))
        def _():
            for k in range(2):
                g = second + k
                chunk_wait(g)

                @pl.when(near & (m == 0))
                def _():
                    across(g).start()

                @pl.when(even)
                def _():
                    beside(g).start()

    early = hub | (near & (m == 0))

    @pl.when(early)
    def _():
        take_first()

    drain(cnt.at[pl.ds(0, KVH - 1)], c_r)
    drain(kvall.at[pl.ds(0, KVH - 1)], k_r)

    def num_send(owner):
        return remote(num.at[owner], numr.at[me], n_s, n_r, owner)

    def q_wait(q):
        @pl.when(q == p)
        def _():
            drain(qall.at[pl.ds(0, KVH - 1)], q_r.at[q])

        @pl.when(q != p)
        def _():
            drain(qall.at[pl.ds(0, KVH)], q_r.at[q])

    diag = lax.broadcasted_iota(jnp.int32, (span, DH), 0) == lax.broadcasted_iota(
        jnp.int32, (span, DH), 1
    )

    def ask(with_self):
        total_rows = PAIR * span
        lane = lax.broadcasted_iota(jnp.int32, (total_rows, rows), 1).astype(jnp.float32)

        @pl.loop(0, planes // PAIR)
        def _(step):
            at_planes = [step * PAIR + k for k in range(PAIR)]
            for q in at_planes:
                q_wait(q)
            queries = jnp.concatenate(
                [qall[pl.ds(q * KVH, KVH)].reshape(span, DH) for q in at_planes], axis=0
            )
            s = [
                lax.dot_general(queries, kvall[j, 0], NT, preferred_element_type=jnp.float32)
                for j in range(KVH)
            ]
            s = [
                jnp.where(lane < cnt[j].astype(jnp.float32)[0:1, :], s[j], -jnp.inf)
                for j in range(KVH)
            ]
            values = [kvall[j, 1] for j in range(KVH)]
            top = [jnp.max(x, axis=1, keepdims=True) for x in s]
            if with_self:
                keys = selfkv[:, 0].reshape(n * tile, DH)
                s2 = lax.dot_general(queries, keys, NT, preferred_element_type=jnp.float32)
                shape = (total_rows, n * tile)
                at = lax.broadcasted_iota(jnp.int32, shape, 1)
                row = lax.broadcasted_iota(jnp.int32, shape, 0)
                shift = tile.bit_length() - 1
                u = (at >> shift) * tokens + (at & (tile - 1))
                t = ((at_planes[0] * span + row) >> shift) * tokens + (row & (tokens - 1))
                s2 = jnp.where(((at & (tile - 1)) < tokens) & (u <= t), s2, -jnp.inf)
                s[-1] = jnp.concatenate([s[-1], s2], axis=1)
                values[-1] = jnp.concatenate(
                    [values[-1], selfkv[:, 1].reshape(n * tile, DH)], axis=0
                )
                top[-1] = jnp.maximum(top[-1], jnp.max(s2, axis=1, keepdims=True))
            e = [jnp.exp2((x - y) * C) for x, y in zip(s, top)]
            part = [jnp.sum(x, axis=1, keepdims=True) for x in e]
            mixed = [
                lax.dot_general(
                    x.astype(jnp.bfloat16), v, NN, preferred_element_type=jnp.float32
                )
                for x, v in zip(e, values)
            ]
            best = functools.reduce(jnp.maximum, top)
            factor = [jnp.exp2((x - best) * C) for x in top]
            total = sum(x * y for x, y in zip(part, factor))
            summed = sum(x * y for x, y in zip(mixed, factor))
            pick = lax.broadcasted_iota(jnp.int32, (TAIL, DH), 0) == 0
            for k, q in enumerate(at_planes):
                cut = slice(k * span, (k + 1) * span)
                line1 = jnp.sum(jnp.where(diag, best[cut], 0.0), axis=0, keepdims=True)
                line2 = jnp.sum(jnp.where(diag, total[cut], 0.0), axis=0, keepdims=True)
                tail = jnp.where(pick, line1, line2)
                for j in range(KVH):
                    owner = q * KVH + j
                    at = k * span + j * tile
                    num[owner, pl.ds(0, tile)] = summed[at : at + tile]
                    num[owner, pl.ds(tile, TAIL)] = tail

                    @pl.when(owner != me)
                    def _():
                        num_send(owner).start()

    @pl.when(is_last)
    def _():
        drain(selfkv.at[pl.ds(0, n - 1)], r_s)
        ask(True)

    @pl.when(jnp.logical_not(is_last))
    def _():
        ask(False)

    numr[me] = num[me]

    @pl.when(jnp.logical_not(early))
    def _():
        take_first()

    @pl.when(jnp.logical_not(is_root))
    def _():
        @pl.loop(0, 2)
        def _(k):
            context(first + k)

    take_second()

    @pl.when(jnp.logical_not(is_root))
    def _():
        @pl.loop(0, 2)
        def _(k):
            context(second + k)

    drain(qall.at[pl.ds(0, n - 1)], q_s)
    drain(cnt.at[pl.ds(0, KVH - 1)], c_s)
    drain(kvall.at[pl.ds(0, KVH - 1)], k_s)

    @pl.when(is_last)
    def _():
        drain(selfkv.at[pl.ds(0, KVH - 1)], f_s)

    @pl.when(jnp.logical_not(is_last))
    def _():
        drain(selfkv.at[pl.ds(0, KVH)], f_s)

    @pl.when(even)
    def _():
        drain(kc.at[:, :, 0], beside_s)

    @pl.when(is_root | (near & (m == 0)))
    def _():
        drain(kc.at[:, :, 0], across_s)

    @pl.when(even & (p > 1))
    def _():
        drain(kc.at[pl.ds(0, 2), :, 0], across_s)

    @pl.when(is_root)
    def _():
        drain(kc.at[:, :, 0], near_s)

    @pl.when(is_root | hub)
    def _():
        for k in range(2):
            drain(qbuf.at[:, pl.ds(0, (planes - 2) * 2 * DH)], far_s.at[k])

    drain(num.at[pl.ds(0, n - 1)], n_s)
    drain(numr.at[pl.ds(0, n - 1)], n_r)


def finish(obuf, numr, ctx_out, ask_out, fin, aout, s_out):
    n, size, _ = numr.shape
    tile = size - TAIL
    tokens = ask_out.shape[0]
    G = tile // tokens
    planes = n // KVH
    span = KVH * tile
    m = lax.axis_index("hst") % KVH
    ctx_copy = pltpu.make_async_copy(obuf, ctx_out, s_out.at[0])
    ctx_copy.start()
    row = lax.broadcasted_iota(jnp.int32, (span, DH), 0)
    lane = lax.broadcasted_iota(jnp.int32, (span, DH), 1)
    diag = lane == (row & (tile - 1)) + m * tile

    def column(line):
        line = jnp.broadcast_to(line, (KVH, tile, DH)).reshape(span, DH)
        return jnp.sum(jnp.where(diag, line, 0.0), axis=1, keepdims=True)

    top, part, mixed = [], [], []
    for q in range(planes):
        at = pl.ds(q * KVH, KVH)
        top.append(column(numr[at, pl.ds(tile, 1)]))
        part.append(column(numr[at, pl.ds(tile + 1, 1)]))
        mixed.append(numr[at, pl.ds(0, tile)].reshape(span, DH))
    best = functools.reduce(jnp.maximum, top)
    factor = [jnp.exp2((x - best) * C) for x in top]
    total = sum(x * y for x, y in zip(part, factor))
    summed = sum(x * y for x, y in zip(mixed, factor))
    fin[...] = summed * (1.0 / total)
    for g in range(KVH):
        for h in range(G):
            at = (g * G + h) * DH
            aout[:, at : at + DH] = fin[pl.ds(g * tile + h * tokens, tokens), :].astype(jnp.bfloat16)
    ask_copy = pltpu.make_async_copy(aout, ask_out, s_out.at[1])
    ask_copy.start()
    ask_copy.wait()
    ctx_copy.wait()


def body(n, ctx_q, ctx_k, ctx_v, ask_q, ask_k, ask_v, valid):
    rows, width = ctx_q.shape
    tokens = ask_q.shape[0]
    G = width // (KVH * DH)
    tile = tokens * G
    planes = n // KVH
    dma = pltpu.SemaphoreType.DMA
    bf = jnp.bfloat16
    f32 = jnp.float32
    large = [
        pltpu.with_memory_space_constraint(x, pltpu.HBM)
        for x in (ctx_q, ctx_k, ctx_v, ask_q, ask_k, ask_v)
    ]
    hbm = pl.BlockSpec(memory_space=pltpu.HBM)
    vmem = pl.BlockSpec(memory_space=pltpu.VMEM)
    obuf, numr = pl.pallas_call(
        functools.partial(kernel, n),
        out_shape=(
            jax.ShapeDtypeStruct(ctx_q.shape, bf),
            jax.ShapeDtypeStruct((n, tile + TAIL, DH), f32),
        ),
        in_specs=[hbm] * 7,
        out_specs=(vmem, vmem),
        scratch_shapes=[
            pltpu.VMEM(ctx_q.shape, bf),
            pltpu.VMEM((KVH, 2, 2, rows, DH), bf),
            pltpu.VMEM((KVH, 2, rows, DH), bf),
            pltpu.VMEM((KVH, tile, DH), bf),
            pltpu.VMEM(ask_q.shape, bf),
            pltpu.VMEM(ask_k.shape, bf),
            pltpu.VMEM(ask_v.shape, bf),
            pltpu.VMEM((KVH, 3, tile, DH), f32),
            pltpu.VMEM((KVH, 3, tile, DH), bf),
            pltpu.VMEM((n, tile, DH), bf),
            pltpu.VMEM((n, 2, tile, DH), bf),
            pltpu.VMEM((n, tile + TAIL, DH), f32),
            pltpu.SMEM((1,), jnp.int32),
            dma,
            dma,
            dma,
            dma,
            dma((4,)),
            dma,
            dma((planes,)),
            dma,
            dma,
            dma,
            dma,
            dma,
            dma,
            dma,
            dma((2,)),
            dma((KVH,)),
            dma,
            dma,
            dma,
            dma,
            pltpu.SemaphoreType.REGULAR,
        ],
        compiler_params=pltpu.CompilerParams(
            collective_id=0, has_side_effects=True, vmem_limit_bytes=16 << 20
        ),
    )(*large, valid)
    return pl.pallas_call(
        finish,
        out_shape=(
            jax.ShapeDtypeStruct(ctx_q.shape, bf),
            jax.ShapeDtypeStruct(ask_q.shape, bf),
        ),
        in_specs=[vmem, vmem],
        out_specs=(hbm, hbm),
        scratch_shapes=[
            pltpu.VMEM((KVH * tile, DH), f32),
            pltpu.VMEM(ask_q.shape, bf),
            dma((2,)),
        ],
        compiler_params=pltpu.CompilerParams(vmem_limit_bytes=8 << 20),
    )(obuf, numr)


def solution(mesh):
    n = mesh.shape["hst"]
    rows = P(("req", "hst"), None)
    return jax.shard_map(
        functools.partial(body, n),
        mesh=mesh,
        in_specs=(rows,) * 6 + (P(("req", "hst")),),
        out_specs=(rows, rows),
        check_vma=False,
    )
```

```python
import functools
import math

import jax
import jax.numpy as jnp
from jax import lax
from jax.experimental import pallas as pl
from jax.experimental.pallas import tpu as pltpu
from jax.sharding import PartitionSpec as P

KVH = 4
DH = 128
PAIR = 2
FULL = 32767.0
TINY = 1e-30
C = math.log2(math.e) / math.sqrt(DH)
NT = (((1,), (1,)), ((), ()))
NN = (((1,), (0,)), ((), ()))


def remote(src, dst, send_sem, recv_sem, target):
    return pltpu.make_async_remote_copy(
        src_ref=src,
        dst_ref=dst,
        send_sem=send_sem,
        recv_sem=recv_sem,
        device_id={"hst": target},
        device_id_type=pl.DeviceIdType.MESH,
    )


def kernel(
    n, ctx_q, ctx_k, ctx_v, ask_q, ask_k, ask_v, valid, obuf, numr, statr,
    qbuf, kc, kvall, cnt, qraw, kraw, vraw, stage, pack, selfpack, qall, selfkv, kself, num, stat,
    count_ref,
    s_kv, s_an, s_q, s_own, s_raw,
    q_s, q_r, k_s, k_r, c_s, c_r, across_s, beside_s, near_s, far_s, a_r, f_s, r_s, n_s, n_r, t_s, t_r, go,
):
    rows = ctx_q.shape[0]
    G = ctx_q.shape[1] // (KVH * DH)
    tokens = ask_q.shape[0]
    tile = pack.shape[1]
    planes = n // KVH
    span = KVH * tile
    me = lax.axis_index("hst")
    p = me // KVH
    m = me % KVH
    is_root = me == 0
    is_last = p == planes - 1
    far = (m + 2) % KVH
    even = m % 2 == 0
    hub = (p == 0) & (m == 2)
    near = p == 1

    barrier = pltpu.get_barrier_semaphore()

    child = (me == 1) | (me == 2) | (me == KVH)

    def signal(sem, target):
        pl.semaphore_signal(
            sem, inc=1, device_id={"hst": target}, device_id_type=pl.DeviceIdType.MESH
        )

    @pl.when(child)
    def _():
        signal(barrier, 0)

    @pl.loop(1, n)
    def _(d):
        target = (me + d) % n

        @pl.when(target != 0)
        def _():
            signal(barrier, target)

    def drain(ref, sem):
        pltpu.make_async_copy(ref, ref, sem).wait()

    def cols(g):
        return pl.ds(pl.multiple_of(g * DH, DH), DH)

    raw_loads = [
        pltpu.make_async_copy(ask_q, qraw, s_raw.at[0]),
        pltpu.make_async_copy(ask_k, kraw, s_raw.at[1]),
        pltpu.make_async_copy(ask_v, vraw, s_raw.at[2]),
        pltpu.make_async_copy(valid, count_ref, s_raw.at[3]),
    ]
    for copy in raw_loads:
        copy.start()

    def load_kv(g, i, half, sem):
        src = (ctx_k, ctx_v)[i]
        return pltpu.make_async_copy(src.at[:, cols(g)], kc.at[g, i, half], sem)

    for g in range(KVH):
        for i in range(2):
            load_kv(g, i, 1, s_kv).start()

    @pl.when(is_root)
    def _():
        for g in range(KVH):
            for i in range(2):
                load_kv(g, i, 0, s_an).start()

    q_load = pltpu.make_async_copy(ctx_q, qbuf, s_q)
    q_load.start()

    own_kv = [
        pltpu.make_async_copy(ctx_k.at[:, cols(m)], kvall.at[m, 0], s_own),
        pltpu.make_async_copy(ctx_v.at[:, cols(m)], kvall.at[m, 1], s_own),
    ]
    for copy in own_kv:
        copy.start()

    for copy in raw_loads:
        copy.wait()
    for g in range(KVH):
        for h in range(G):
            at = (g * G + h) * DH
            stage[g, pl.ds(h * tokens, tokens), :] = qraw[:, at : at + DH].astype(jnp.float32)
        for i, raw in ((0, kraw), (1, vraw)):
            selfpack[g, pl.ds(i * tokens, tokens), :] = raw[:, g * DH : g * DH + DH].astype(
                jnp.float32
            )
    pack[...] = stage[...].astype(jnp.bfloat16)
    cnt[m] = jnp.full((tile, DH), count_ref[0].astype(jnp.float32)).astype(jnp.bfloat16)
    qall[me] = pack[m]

    @pl.when(is_last)
    def _():
        selfkv[me] = selfpack[m]

    drain(kc.at[:, :, 1], s_kv)
    drain(kvall.at[m], s_own)
    q_load.wait()

    def context(g):
        count = cnt[m].astype(jnp.float32)[0:1, :]
        row = lax.broadcasted_iota(jnp.int32, (rows, rows), 0)
        lane = lax.broadcasted_iota(jnp.int32, (rows, rows), 1)
        own = (lane <= row) & (lane.astype(jnp.float32) < count)
        outer = jnp.broadcast_to(me, (rows, rows)) > 0
        visible = jnp.concatenate([outer, own], axis=1)
        kept = lax.broadcasted_iota(jnp.int32, (rows, DH), 0).astype(jnp.float32) < count
        keys = kc[g, 0].reshape(2 * rows, DH)
        values = kc[g, 1].reshape(2 * rows, DH)
        at = [pl.ds(pl.multiple_of((g * G + k) * DH, DH), DH) for k in range(G)]
        s = [
            lax.dot_general(qbuf[:, x], keys, NT, preferred_element_type=jnp.float32)
            for x in at
        ]
        s = [jnp.where(visible, x, -jnp.inf) for x in s]
        top = [jnp.max(x, axis=1, keepdims=True) for x in s]
        e = [jnp.exp2((x - y) * C) for x, y in zip(s, top)]
        total = [jnp.sum(x, axis=1, keepdims=True) for x in e]
        mixed = [
            lax.dot_general(x.astype(jnp.bfloat16), values, NN, preferred_element_type=jnp.float32)
            for x in e
        ]
        for k in range(G):
            out = jnp.where(kept, mixed[k] * (1.0 / total[k]), 0.0)
            obuf[:, at[k]] = out.astype(jnp.bfloat16)

    def chunk_send(g, sem, target):
        piece = kc.at[g, :, 0]
        return remote(piece, piece, sem, a_r.at[g], target)

    def across(g):
        return chunk_send(g, across_s, p * KVH + far)

    def beside(g):
        return chunk_send(g, beside_s, p * KVH + m + 1)

    def along_near(g):
        return chunk_send(g, near_s, KVH)

    def along_far(g, k, q):
        return chunk_send(g, far_s.at[k], q * KVH + m)

    @pl.when(is_root)
    def _():
        drain(kc.at[:, :, 0], s_an)

        @pl.loop(0, 2)
        def _(g):
            context(g)

        pl.semaphore_wait(barrier, 3)
        for g in (2, 3):
            across(g).start()
        for g in range(KVH):
            along_near(g).start()
        for g in range(KVH):
            beside(g).start()
        for g in (0, 1):
            across(g).start()

        @pl.loop(2, KVH)
        def _(g):
            context(g)

        pl.semaphore_wait(go, 1)

    @pl.when(jnp.logical_not(is_root))
    def _():
        pl.semaphore_wait(barrier, n - 1)

    @pl.when(me == 1)
    def _():
        signal(go, 0)

    def q_send(d):
        target = (me + n - d) % n
        return remote(pack.at[target % KVH], qall.at[me], q_s, q_r.at[p], target)

    def cnt_send(d):
        g = (m + d) % KVH
        return remote(cnt.at[m], cnt.at[m], c_s, c_r, p * KVH + g)

    def kv_send(d):
        g = (m + d) % KVH
        return remote(kc.at[g, :, 1], kvall.at[m], k_s, k_r, p * KVH + g)

    @pl.when(p > 0)
    def _():
        for d in (2, 3, 1):
            kv_send(d).start()
            cnt_send(d).start()

    @pl.loop(1, n)
    def _(d):
        q_send(d).start()

    def self_send(g):
        return remote(selfpack.at[g], selfkv.at[me], f_s, r_s, n - KVH + g)

    for g in range(KVH):
        @pl.when(me != n - KVH + g)
        def _():
            self_send(g).start()

    @pl.when(p == 0)
    def _():
        for d in (2, 3, 1):
            kv_send(d).start()
            cnt_send(d).start()

    @pl.when(is_root)
    def _():
        for q in range(planes - 1, 1, -1):
            for g in (0, 1):
                along_far(g, g, q).start()

    first = jnp.where(near, 0, m // 2 * 2)
    second = 2 - first

    def chunk_wait(g):
        drain(kc.at[g, :, 0], a_r.at[g])

    def take_first():
        @pl.when(jnp.logical_not(is_root))
        def _():
            for k in range(2):
                g = first + k
                chunk_wait(g)

                @pl.when(hub)
                def _():
                    for q in range(planes - 1, 1, -1):
                        along_far(g, k, q).start()

                @pl.when((near & (m == 0)) | (even & (p > 1)))
                def _():
                    across(g).start()

                @pl.when(even)
                def _():
                    beside(g).start()

    def take_second():
        @pl.when(jnp.logical_not(is_root))
        def _():
            for k in range(2):
                g = second + k
                chunk_wait(g)

                @pl.when(near & (m == 0))
                def _():
                    across(g).start()

                @pl.when(even)
                def _():
                    beside(g).start()

    early = hub | (near & (m == 0))

    @pl.when(early)
    def _():
        take_first()

    drain(cnt.at[pl.ds(0, KVH - 1)], c_r)
    drain(kvall.at[pl.ds(0, KVH - 1)], k_r)

    def num_send(owner):
        return remote(num.at[owner], numr.at[me], n_s, n_r, owner)

    def stat_send(owner):
        return remote(stat.at[owner], statr.at[me], t_s, t_r, owner)

    def q_wait(q):
        @pl.when(q == p)
        def _():
            drain(qall.at[pl.ds(0, KVH - 1)], q_r.at[q])

        @pl.when(q != p)
        def _():
            drain(qall.at[pl.ds(0, KVH)], q_r.at[q])

    row = lax.broadcasted_iota(jnp.int32, (span, DH), 0)
    lane = lax.broadcasted_iota(jnp.int32, (span, DH), 1)
    diag, shifted = lane == row, lane == row + span

    def line(mask, x):
        return jnp.sum(jnp.where(mask, x, 0.0), axis=0, keepdims=True)

    def ask(with_self):
        total_rows = PAIR * span
        lane = lax.broadcasted_iota(jnp.int32, (total_rows, rows), 1).astype(jnp.float32)

        @pl.loop(0, planes // PAIR)
        def _(step):
            at_planes = [step * PAIR + k for k in range(PAIR)]
            for q in at_planes:
                q_wait(q)
            queries = jnp.concatenate(
                [qall[pl.ds(q * KVH, KVH)].reshape(span, DH) for q in at_planes], axis=0
            )
            s = [
                lax.dot_general(queries, kvall[j, 0], NT, preferred_element_type=jnp.float32)
                for j in range(KVH)
            ]
            s = [
                jnp.where(lane < cnt[j].astype(jnp.float32)[0:1, :], s[j], -jnp.inf)
                for j in range(KVH)
            ]
            values = [kvall[j, 1] for j in range(KVH)]
            top = [jnp.max(x, axis=1, keepdims=True) for x in s]
            if with_self:
                keys = kself[0].astype(jnp.bfloat16)
                s2 = lax.dot_general(queries, keys, NT, preferred_element_type=jnp.float32)
                u = lax.broadcasted_iota(jnp.int32, s2.shape, 1)
                row = lax.broadcasted_iota(jnp.int32, s2.shape, 0)
                shift = tile.bit_length() - 1
                t = ((at_planes[0] * span + row) >> shift) * tokens + (row & (tokens - 1))
                s2 = jnp.where(u <= t, s2, -jnp.inf)
                s[-1] = jnp.concatenate([s[-1], s2], axis=1)
                values[-1] = jnp.concatenate([values[-1], kself[1].astype(jnp.bfloat16)], axis=0)
                top[-1] = jnp.maximum(top[-1], jnp.max(s2, axis=1, keepdims=True))
            e = [jnp.exp2((x - y) * C) for x, y in zip(s, top)]
            part = [jnp.sum(x, axis=1, keepdims=True) for x in e]
            mixed = [
                lax.dot_general(
                    x.astype(jnp.bfloat16), v, NN, preferred_element_type=jnp.float32
                )
                for x, v in zip(e, values)
            ]
            best = functools.reduce(jnp.maximum, top)
            factor = [jnp.exp2((x - best) * C) for x in top]
            total = sum(x * y for x, y in zip(part, factor))
            summed = sum(x * y for x, y in zip(mixed, factor))
            size = jnp.maximum(jnp.max(jnp.abs(summed), axis=1, keepdims=True), TINY)
            coded = jnp.round(summed * (FULL / size)).astype(jnp.int32).astype(jnp.int16)
            for k, q in enumerate(at_planes):
                cut = slice(k * span, (k + 1) * span)
                line1 = line(diag, best[cut]) + line(shifted, total[cut])
                line2 = line(diag, size[cut])
                for j in range(KVH):
                    owner = q * KVH + j
                    at = k * span + j * tile
                    num[owner] = coded[at : at + tile]
                    stat[owner, pl.ds(0, 1)] = line1
                    stat[owner, pl.ds(1, 1)] = line2

                    @pl.when(owner != me)
                    def _():
                        num_send(owner).start()
                        stat_send(owner).start()

    @pl.when(is_last)
    def _():
        drain(selfkv.at[pl.ds(0, n - 1)], r_s)
        for source in range(n):
            for i in range(2):
                kself[i, pl.ds(source * tokens, tokens)] = selfkv[source, pl.ds(i * tokens, tokens)]
        ask(True)

    @pl.when(jnp.logical_not(is_last))
    def _():
        ask(False)

    numr[me] = num[me]
    statr[me] = stat[me]

    @pl.when(jnp.logical_not(early))
    def _():
        take_first()

    @pl.when(jnp.logical_not(is_root))
    def _():
        @pl.loop(0, 2)
        def _(k):
            context(first + k)

    take_second()

    @pl.when(jnp.logical_not(is_root))
    def _():
        @pl.loop(0, 2)
        def _(k):
            context(second + k)

    drain(qall.at[pl.ds(0, n - 1)], q_s)
    drain(cnt.at[pl.ds(0, KVH - 1)], c_s)
    drain(kvall.at[pl.ds(0, KVH - 1)], k_s)

    @pl.when(is_last)
    def _():
        drain(selfkv.at[pl.ds(0, KVH - 1)], f_s)

    @pl.when(jnp.logical_not(is_last))
    def _():
        drain(selfkv.at[pl.ds(0, KVH)], f_s)

    @pl.when(even)
    def _():
        drain(kc.at[:, :, 0], beside_s)

    @pl.when(is_root | (near & (m == 0)))
    def _():
        drain(kc.at[:, :, 0], across_s)

    @pl.when(even & (p > 1))
    def _():
        drain(kc.at[pl.ds(0, 2), :, 0], across_s)

    @pl.when(is_root)
    def _():
        drain(kc.at[:, :, 0], near_s)

    @pl.when(is_root | hub)
    def _():
        for k in range(2):
            drain(qbuf.at[:, pl.ds(0, (planes - 2) * 2 * DH)], far_s.at[k])

    drain(num.at[pl.ds(0, n - 1)], n_s)
    drain(stat.at[pl.ds(0, n - 1)], t_s)
    drain(numr.at[pl.ds(0, n - 1)], n_r)
    drain(statr.at[pl.ds(0, n - 1)], t_r)


def finish(obuf, numr, statr, ctx_out, ask_out, fin, aout, s_out):
    n, tile, _ = numr.shape
    tokens = ask_out.shape[0]
    G = tile // tokens
    planes = n // KVH
    span = KVH * tile
    m = lax.axis_index("hst") % KVH
    ctx_copy = pltpu.make_async_copy(obuf, ctx_out, s_out.at[0])
    ctx_copy.start()
    row = lax.broadcasted_iota(jnp.int32, (span, DH), 0)
    lane = lax.broadcasted_iota(jnp.int32, (span, DH), 1)
    place = (row & (tile - 1)) + m * tile
    diag, shifted = lane == place, lane == place + span

    def column(q, k, mask):
        line = statr[pl.ds(q * KVH, KVH), pl.ds(k, 1)]
        line = jnp.broadcast_to(line, (KVH, tile, DH)).reshape(span, DH)
        return jnp.sum(jnp.where(mask, line, 0.0), axis=1, keepdims=True)

    top, part, mixed = [], [], []
    for q in range(planes):
        top.append(column(q, 0, diag))
        part.append(column(q, 0, shifted))
        coded = numr[pl.ds(q * KVH, KVH)].reshape(span, DH).astype(jnp.int32)
        mixed.append(coded.astype(jnp.float32) * (column(q, 1, diag) * (1.0 / FULL)))
    best = functools.reduce(jnp.maximum, top)
    factor = [jnp.exp2((x - best) * C) for x in top]
    total = sum(x * y for x, y in zip(part, factor))
    summed = sum(x * y for x, y in zip(mixed, factor))
    fin[...] = summed * (1.0 / total)
    for g in range(KVH):
        for h in range(G):
            at = (g * G + h) * DH
            aout[:, at : at + DH] = fin[pl.ds(g * tile + h * tokens, tokens), :].astype(jnp.bfloat16)
    ask_copy = pltpu.make_async_copy(aout, ask_out, s_out.at[1])
    ask_copy.start()
    ask_copy.wait()
    ctx_copy.wait()


def body(n, ctx_q, ctx_k, ctx_v, ask_q, ask_k, ask_v, valid):
    rows, width = ctx_q.shape
    tokens = ask_q.shape[0]
    G = width // (KVH * DH)
    tile = tokens * G
    planes = n // KVH
    dma = pltpu.SemaphoreType.DMA
    bf = jnp.bfloat16
    f32 = jnp.float32
    large = [
        pltpu.with_memory_space_constraint(x, pltpu.HBM)
        for x in (ctx_q, ctx_k, ctx_v, ask_q, ask_k, ask_v)
    ]
    hbm = pl.BlockSpec(memory_space=pltpu.HBM)
    vmem = pl.BlockSpec(memory_space=pltpu.VMEM)
    obuf, numr, statr = pl.pallas_call(
        functools.partial(kernel, n),
        out_shape=(
            jax.ShapeDtypeStruct(ctx_q.shape, bf),
            jax.ShapeDtypeStruct((n, tile, DH), jnp.int16),
            jax.ShapeDtypeStruct((n, 2, DH), f32),
        ),
        in_specs=[hbm] * 7,
        out_specs=(vmem,) * 3,
        scratch_shapes=[
            pltpu.VMEM(ctx_q.shape, bf),
            pltpu.VMEM((KVH, 2, 2, rows, DH), bf),
            pltpu.VMEM((KVH, 2, rows, DH), bf),
            pltpu.VMEM((KVH, tile, DH), bf),
            pltpu.VMEM(ask_q.shape, bf),
            pltpu.VMEM(ask_k.shape, bf),
            pltpu.VMEM(ask_v.shape, bf),
            pltpu.VMEM((KVH, tile, DH), f32),
            pltpu.VMEM((KVH, tile, DH), bf),
            pltpu.VMEM((KVH, 2 * tokens, DH), f32),
            pltpu.VMEM((n, tile, DH), bf),
            pltpu.VMEM((n, 2 * tokens, DH), f32),
            pltpu.VMEM((2, n * tokens, DH), f32),
            pltpu.VMEM((n, tile, DH), jnp.int16),
            pltpu.VMEM((n, 2, DH), f32),
            pltpu.SMEM((1,), jnp.int32),
            dma,
            dma,
            dma,
            dma,
            dma((4,)),
            dma,
            dma((planes,)),
            dma,
            dma,
            dma,
            dma,
            dma,
            dma,
            dma,
            dma((2,)),
            dma((KVH,)),
            dma,
            dma,
            dma,
            dma,
            dma,
            dma,
            pltpu.SemaphoreType.REGULAR,
        ],
        compiler_params=pltpu.CompilerParams(
            collective_id=0, has_side_effects=True, vmem_limit_bytes=16 << 20
        ),
    )(*large, valid)
    return pl.pallas_call(
        finish,
        out_shape=(
            jax.ShapeDtypeStruct(ctx_q.shape, bf),
            jax.ShapeDtypeStruct(ask_q.shape, bf),
        ),
        in_specs=[vmem] * 3,
        out_specs=(hbm, hbm),
        scratch_shapes=[
            pltpu.VMEM((KVH * tile, DH), f32),
            pltpu.VMEM(ask_q.shape, bf),
            dma((2,)),
        ],
        compiler_params=pltpu.CompilerParams(vmem_limit_bytes=8 << 20),
    )(obuf, numr, statr)


def solution(mesh):
    n = mesh.shape["hst"]
    rows = P(("req", "hst"), None)
    return jax.shard_map(
        functools.partial(body, n),
        mesh=mesh,
        in_specs=(rows,) * 6 + (P(("req", "hst")),),
        out_specs=(rows, rows),
        check_vma=False,
    )
```

```python
import functools
import math

import jax
import jax.numpy as jnp
from jax import lax
from jax.experimental import pallas as pl
from jax.experimental.pallas import tpu as pltpu
from jax.sharding import PartitionSpec as P

KVH = 4
DH = 128
PAIR = 2
FULL = 32767.0
TINY = 1e-30
C = math.log2(math.e) / math.sqrt(DH)
NT = (((1,), (1,)), ((), ()))
NN = (((1,), (0,)), ((), ()))


def remote(src, dst, send_sem, recv_sem, target):
    return pltpu.make_async_remote_copy(
        src_ref=src,
        dst_ref=dst,
        send_sem=send_sem,
        recv_sem=recv_sem,
        device_id={"hst": target},
        device_id_type=pl.DeviceIdType.MESH,
    )


def kernel(
    n, ctx_q, ctx_k, ctx_v, ask_q, ask_k, ask_v, valid, obuf, numr, statr,
    qbuf, kc, kvall, cnt, qraw, kraw, vraw, stage, pack, selfpack, qall, selfkv, kself, num, stat,
    count_ref,
    s_kv, s_an, s_q, s_own, s_raw,
    q_s, q_r, k_s, k_r, c_s, c_r, across_s, beside_s, near_s, far_s, a_r, f_s, r_s, n_s, n_r, t_s, t_r, go,
):
    rows = ctx_q.shape[0]
    G = ctx_q.shape[1] // (KVH * DH)
    tokens = ask_q.shape[0]
    tile = pack.shape[1]
    planes = n // KVH
    span = KVH * tile
    me = lax.axis_index("hst")
    p = me // KVH
    m = me % KVH
    is_root = me == 0
    is_last = p == planes - 1
    far = (m + 2) % KVH
    even = m % 2 == 0
    hub = (p == 0) & (m == 2)
    near = p == 1

    barrier = pltpu.get_barrier_semaphore()

    child = (me == 1) | (me == 2) | (me == KVH)

    def signal(sem, target):
        pl.semaphore_signal(
            sem, inc=1, device_id={"hst": target}, device_id_type=pl.DeviceIdType.MESH
        )

    @pl.when(child)
    def _():
        signal(barrier, 0)

    @pl.loop(1, n)
    def _(d):
        target = (me + d) % n

        @pl.when(target != 0)
        def _():
            signal(barrier, target)

    def drain(ref, sem):
        pltpu.make_async_copy(ref, ref, sem).wait()

    def cols(g):
        return pl.ds(pl.multiple_of(g * DH, DH), DH)

    raw_loads = [
        pltpu.make_async_copy(ask_q, qraw, s_raw.at[0]),
        pltpu.make_async_copy(ask_k, kraw, s_raw.at[1]),
        pltpu.make_async_copy(ask_v, vraw, s_raw.at[2]),
        pltpu.make_async_copy(valid, count_ref, s_raw.at[3]),
    ]
    for copy in raw_loads:
        copy.start()

    def load_kv(g, i, half, sem):
        src = (ctx_k, ctx_v)[i]
        return pltpu.make_async_copy(src.at[:, cols(g)], kc.at[g, i, half], sem)

    for g in range(KVH):
        for i in range(2):
            load_kv(g, i, 1, s_kv).start()

    @pl.when(is_root)
    def _():
        for g in range(KVH):
            for i in range(2):
                load_kv(g, i, 0, s_an).start()

    q_load = pltpu.make_async_copy(ctx_q, qbuf, s_q)
    q_load.start()

    own_kv = [
        pltpu.make_async_copy(ctx_k.at[:, cols(m)], kvall.at[m, 0], s_own),
        pltpu.make_async_copy(ctx_v.at[:, cols(m)], kvall.at[m, 1], s_own),
    ]
    for copy in own_kv:
        copy.start()

    for copy in raw_loads:
        copy.wait()
    for g in range(KVH):
        for h in range(G):
            at = (g * G + h) * DH
            stage[g, pl.ds(h * tokens, tokens), :] = qraw[:, at : at + DH].astype(jnp.float32)
        for i, raw in ((0, kraw), (1, vraw)):
            selfpack[g, pl.ds(i * tokens, tokens), :] = raw[:, g * DH : g * DH + DH].astype(
                jnp.float32
            )
    pack[...] = stage[...].astype(jnp.bfloat16)
    cnt[m] = jnp.full((tile, DH), count_ref[0].astype(jnp.float32)).astype(jnp.bfloat16)
    qall[me] = pack[m]

    @pl.when(is_last)
    def _():
        selfkv[me] = selfpack[m]

    drain(kc.at[:, :, 1], s_kv)
    drain(kvall.at[m], s_own)
    q_load.wait()

    def context(g):
        count = cnt[m].astype(jnp.float32)[0:1, :]
        row = lax.broadcasted_iota(jnp.int32, (rows, rows), 0)
        lane = lax.broadcasted_iota(jnp.int32, (rows, rows), 1)
        own = (lane <= row) & (lane.astype(jnp.float32) < count)
        outer = jnp.broadcast_to(me, (rows, rows)) > 0
        visible = jnp.concatenate([outer, own], axis=1)
        kept = lax.broadcasted_iota(jnp.int32, (rows, DH), 0).astype(jnp.float32) < count
        keys = kc[g, 0].reshape(2 * rows, DH)
        values = kc[g, 1].reshape(2 * rows, DH)
        at = [pl.ds(pl.multiple_of((g * G + k) * DH, DH), DH) for k in range(G)]
        s = [
            lax.dot_general(qbuf[:, x], keys, NT, preferred_element_type=jnp.float32)
            for x in at
        ]
        s = [jnp.where(visible, x, -jnp.inf) for x in s]
        top = [jnp.max(x, axis=1, keepdims=True) for x in s]
        e = [jnp.exp2((x - y) * C) for x, y in zip(s, top)]
        total = [jnp.sum(x, axis=1, keepdims=True) for x in e]
        mixed = [
            lax.dot_general(x.astype(jnp.bfloat16), values, NN, preferred_element_type=jnp.float32)
            for x in e
        ]
        for k in range(G):
            out = jnp.where(kept, mixed[k] * (1.0 / total[k]), 0.0)
            obuf[:, at[k]] = out.astype(jnp.bfloat16)

    def chunk_send(g, sem, target):
        piece = kc.at[g, :, 0]
        return remote(piece, piece, sem, a_r.at[g], target)

    def across(g):
        return chunk_send(g, across_s, p * KVH + far)

    def beside(g):
        return chunk_send(g, beside_s, p * KVH + m + 1)

    def along_near(g):
        return chunk_send(g, near_s, KVH)

    def along_far(g, q):
        return chunk_send(g, far_s.at[g], q * KVH + m)

    @pl.when(is_root)
    def _():
        drain(kc.at[:, :, 0], s_an)

        pl.semaphore_wait(barrier, 3)
        for g in range(KVH):
            across(g).start()
            along_near(g).start()
            beside(g).start()

        pl.semaphore_wait(go, 1)

    @pl.when(jnp.logical_not(is_root))
    def _():
        pl.semaphore_wait(barrier, n - 1)

    @pl.when(me == 1)
    def _():
        signal(go, 0)

    def q_send(target):
        return remote(pack.at[target % KVH], qall.at[me], q_s, q_r.at[p], target)

    def self_send(g):
        return remote(selfpack.at[g], selfkv.at[me], f_s, r_s, n - KVH + g)

    def cnt_send(d):
        g = (m + d) % KVH
        return remote(cnt.at[m], cnt.at[m], c_s, c_r, p * KVH + g)

    def kv_send(d):
        g = (m + d) % KVH
        return remote(kc.at[g, :, 1], kvall.at[m], k_s, k_r, p * KVH + g)

    @pl.when(p > 0)
    def _():
        for d in (2, 3, 1):
            kv_send(d).start()
            cnt_send(d).start()

    for g in range(KVH):
        @pl.when(me != n - KVH + g)
        def _():
            q_send(n - KVH + g).start()
            self_send(g).start()

    @pl.loop(KVH, n)
    def _(i):
        target = n - 1 - i

        @pl.when(target != me)
        def _():
            q_send(target).start()

    @pl.when(p == 0)
    def _():
        for d in (2, 3, 1):
            kv_send(d).start()
            cnt_send(d).start()

    @pl.when(is_root)
    def _():
        for q in range(2, planes):
            for g in range(KVH):
                along_far(g, q).start()

    @pl.when(is_root)
    def _():
        @pl.loop(0, KVH)
        def _(g):
            context(g)

    def take(g):
        drain(kc.at[g, :, 0], a_r.at[g])

        @pl.when(hub)
        def _():
            for q in range(2, planes):
                along_far(g, q).start()

        @pl.when(near & (m == 0))
        def _():
            across(g).start()

        @pl.when(even)
        def _():
            beside(g).start()

    early = hub | (near & (m == 0))

    @pl.when(early)
    def _():
        @pl.loop(0, KVH)
        def _(g):
            take(g)

    drain(cnt.at[pl.ds(0, KVH - 1)], c_r)
    drain(kvall.at[pl.ds(0, KVH - 1)], k_r)

    def num_send(owner):
        return remote(num.at[owner], numr.at[me], n_s, n_r, owner)

    def stat_send(owner):
        return remote(stat.at[owner], statr.at[me], t_s, t_r, owner)

    def q_wait(q):
        @pl.when(q == p)
        def _():
            drain(qall.at[pl.ds(0, KVH - 1)], q_r.at[q])

        @pl.when(q != p)
        def _():
            drain(qall.at[pl.ds(0, KVH)], q_r.at[q])

    row = lax.broadcasted_iota(jnp.int32, (span, DH), 0)
    lane = lax.broadcasted_iota(jnp.int32, (span, DH), 1)
    diag, shifted = lane == row, lane == row + span

    def line(mask, x):
        return jnp.sum(jnp.where(mask, x, 0.0), axis=0, keepdims=True)

    def ask(with_self):
        total_rows = PAIR * span
        lane = lax.broadcasted_iota(jnp.int32, (total_rows, rows), 1).astype(jnp.float32)

        @pl.loop(0, planes // PAIR)
        def _(step):
            at_planes = [step * PAIR + k for k in range(PAIR)]
            for q in at_planes:
                q_wait(q)
            queries = jnp.concatenate(
                [qall[pl.ds(q * KVH, KVH)].reshape(span, DH) for q in at_planes], axis=0
            )
            s = [
                lax.dot_general(queries, kvall[j, 0], NT, preferred_element_type=jnp.float32)
                for j in range(KVH)
            ]
            s = [
                jnp.where(lane < cnt[j].astype(jnp.float32)[0:1, :], s[j], -jnp.inf)
                for j in range(KVH)
            ]
            values = [kvall[j, 1] for j in range(KVH)]
            top = [jnp.max(x, axis=1, keepdims=True) for x in s]
            if with_self:
                keys = kself[0].astype(jnp.bfloat16)
                s2 = lax.dot_general(queries, keys, NT, preferred_element_type=jnp.float32)
                u = lax.broadcasted_iota(jnp.int32, s2.shape, 1)
                row = lax.broadcasted_iota(jnp.int32, s2.shape, 0)
                shift = tile.bit_length() - 1
                t = ((at_planes[0] * span + row) >> shift) * tokens + (row & (tokens - 1))
                s2 = jnp.where(u <= t, s2, -jnp.inf)
                s[-1] = jnp.concatenate([s[-1], s2], axis=1)
                values[-1] = jnp.concatenate([values[-1], kself[1].astype(jnp.bfloat16)], axis=0)
                top[-1] = jnp.maximum(top[-1], jnp.max(s2, axis=1, keepdims=True))
            e = [jnp.exp2((x - y) * C) for x, y in zip(s, top)]
            part = [jnp.sum(x, axis=1, keepdims=True) for x in e]
            mixed = [
                lax.dot_general(
                    x.astype(jnp.bfloat16), v, NN, preferred_element_type=jnp.float32
                )
                for x, v in zip(e, values)
            ]
            best = functools.reduce(jnp.maximum, top)
            factor = [jnp.exp2((x - best) * C) for x in top]
            total = sum(x * y for x, y in zip(part, factor))
            summed = sum(x * y for x, y in zip(mixed, factor))
            size = jnp.maximum(jnp.max(jnp.abs(summed), axis=1, keepdims=True), TINY)
            coded = jnp.round(summed * (FULL / size)).astype(jnp.int32).astype(jnp.int16)
            for k, q in enumerate(at_planes):
                cut = slice(k * span, (k + 1) * span)
                line1 = line(diag, best[cut]) + line(shifted, total[cut])
                line2 = line(diag, size[cut])
                for j in range(KVH):
                    owner = q * KVH + j
                    at = k * span + j * tile
                    num[owner] = coded[at : at + tile]
                    stat[owner, pl.ds(0, 1)] = line1
                    stat[owner, pl.ds(1, 1)] = line2

                    @pl.when(owner != me)
                    def _():
                        num_send(owner).start()
                        stat_send(owner).start()

    @pl.when(is_last)
    def _():
        drain(selfkv.at[pl.ds(0, n - 1)], r_s)
        for source in range(n):
            for i in range(2):
                kself[i, pl.ds(source * tokens, tokens)] = selfkv[source, pl.ds(i * tokens, tokens)]
        ask(True)

    @pl.when(jnp.logical_not(is_last))
    def _():
        ask(False)

    numr[me] = num[me]
    statr[me] = stat[me]

    @pl.when(jnp.logical_not(is_root))
    def _():
        @pl.loop(0, KVH)
        def _(g):
            @pl.when(jnp.logical_not(early))
            def _():
                take(g)

            context(g)

    drain(qall.at[pl.ds(0, n - 1)], q_s)
    drain(cnt.at[pl.ds(0, KVH - 1)], c_s)
    drain(kvall.at[pl.ds(0, KVH - 1)], k_s)

    @pl.when(is_last)
    def _():
        drain(selfkv.at[pl.ds(0, KVH - 1)], f_s)

    @pl.when(jnp.logical_not(is_last))
    def _():
        drain(selfkv.at[pl.ds(0, KVH)], f_s)

    @pl.when(even)
    def _():
        drain(kc.at[:, :, 0], beside_s)

    @pl.when(is_root | (near & (m == 0)))
    def _():
        drain(kc.at[:, :, 0], across_s)

    @pl.when(is_root)
    def _():
        drain(kc.at[:, :, 0], near_s)

    @pl.when(is_root | hub)
    def _():
        for g in range(KVH):
            drain(qbuf.at[:, pl.ds(0, (planes - 2) * 2 * DH)], far_s.at[g])

    drain(num.at[pl.ds(0, n - 1)], n_s)
    drain(stat.at[pl.ds(0, n - 1)], t_s)
    drain(numr.at[pl.ds(0, n - 1)], n_r)
    drain(statr.at[pl.ds(0, n - 1)], t_r)


def finish(obuf, numr, statr, ctx_out, ask_out, fin, aout, s_out):
    n, tile, _ = numr.shape
    tokens = ask_out.shape[0]
    G = tile // tokens
    planes = n // KVH
    span = KVH * tile
    m = lax.axis_index("hst") % KVH
    ctx_copy = pltpu.make_async_copy(obuf, ctx_out, s_out.at[0])
    ctx_copy.start()
    row = lax.broadcasted_iota(jnp.int32, (span, DH), 0)
    lane = lax.broadcasted_iota(jnp.int32, (span, DH), 1)
    place = (row & (tile - 1)) + m * tile
    diag, shifted = lane == place, lane == place + span

    def column(q, k, mask):
        line = statr[pl.ds(q * KVH, KVH), pl.ds(k, 1)]
        line = jnp.broadcast_to(line, (KVH, tile, DH)).reshape(span, DH)
        return jnp.sum(jnp.where(mask, line, 0.0), axis=1, keepdims=True)

    top, part, mixed = [], [], []
    for q in range(planes):
        top.append(column(q, 0, diag))
        part.append(column(q, 0, shifted))
        coded = numr[pl.ds(q * KVH, KVH)].reshape(span, DH).astype(jnp.int32)
        mixed.append(coded.astype(jnp.float32) * (column(q, 1, diag) * (1.0 / FULL)))
    best = functools.reduce(jnp.maximum, top)
    factor = [jnp.exp2((x - best) * C) for x in top]
    total = sum(x * y for x, y in zip(part, factor))
    summed = sum(x * y for x, y in zip(mixed, factor))
    fin[...] = summed * (1.0 / total)
    for g in range(KVH):
        for h in range(G):
            at = (g * G + h) * DH
            aout[:, at : at + DH] = fin[pl.ds(g * tile + h * tokens, tokens), :].astype(jnp.bfloat16)
    ask_copy = pltpu.make_async_copy(aout, ask_out, s_out.at[1])
    ask_copy.start()
    ask_copy.wait()
    ctx_copy.wait()


def body(n, ctx_q, ctx_k, ctx_v, ask_q, ask_k, ask_v, valid):
    rows, width = ctx_q.shape
    tokens = ask_q.shape[0]
    G = width // (KVH * DH)
    tile = tokens * G
    planes = n // KVH
    dma = pltpu.SemaphoreType.DMA
    bf = jnp.bfloat16
    f32 = jnp.float32
    large = [
        pltpu.with_memory_space_constraint(x, pltpu.HBM)
        for x in (ctx_q, ctx_k, ctx_v, ask_q, ask_k, ask_v)
    ]
    hbm = pl.BlockSpec(memory_space=pltpu.HBM)
    vmem = pl.BlockSpec(memory_space=pltpu.VMEM)
    obuf, numr, statr = pl.pallas_call(
        functools.partial(kernel, n),
        out_shape=(
            jax.ShapeDtypeStruct(ctx_q.shape, bf),
            jax.ShapeDtypeStruct((n, tile, DH), jnp.int16),
            jax.ShapeDtypeStruct((n, 2, DH), f32),
        ),
        in_specs=[hbm] * 7,
        out_specs=(vmem,) * 3,
        scratch_shapes=[
            pltpu.VMEM(ctx_q.shape, bf),
            pltpu.VMEM((KVH, 2, 2, rows, DH), bf),
            pltpu.VMEM((KVH, 2, rows, DH), bf),
            pltpu.VMEM((KVH, tile, DH), bf),
            pltpu.VMEM(ask_q.shape, bf),
            pltpu.VMEM(ask_k.shape, bf),
            pltpu.VMEM(ask_v.shape, bf),
            pltpu.VMEM((KVH, tile, DH), f32),
            pltpu.VMEM((KVH, tile, DH), bf),
            pltpu.VMEM((KVH, 2 * tokens, DH), f32),
            pltpu.VMEM((n, tile, DH), bf),
            pltpu.VMEM((n, 2 * tokens, DH), f32),
            pltpu.VMEM((2, n * tokens, DH), f32),
            pltpu.VMEM((n, tile, DH), jnp.int16),
            pltpu.VMEM((n, 2, DH), f32),
            pltpu.SMEM((1,), jnp.int32),
            dma,
            dma,
            dma,
            dma,
            dma((4,)),
            dma,
            dma((planes,)),
            dma,
            dma,
            dma,
            dma,
            dma,
            dma,
            dma,
            dma((KVH,)),
            dma((KVH,)),
            dma,
            dma,
            dma,
            dma,
            dma,
            dma,
            pltpu.SemaphoreType.REGULAR,
        ],
        compiler_params=pltpu.CompilerParams(
            collective_id=0, has_side_effects=True, vmem_limit_bytes=16 << 20
        ),
    )(*large, valid)
    return pl.pallas_call(
        finish,
        out_shape=(
            jax.ShapeDtypeStruct(ctx_q.shape, bf),
            jax.ShapeDtypeStruct(ask_q.shape, bf),
        ),
        in_specs=[vmem] * 3,
        out_specs=(hbm, hbm),
        scratch_shapes=[
            pltpu.VMEM((KVH * tile, DH), f32),
            pltpu.VMEM(ask_q.shape, bf),
            dma((2,)),
        ],
        compiler_params=pltpu.CompilerParams(vmem_limit_bytes=8 << 20),
    )(obuf, numr, statr)


def solution(mesh):
    n = mesh.shape["hst"]
    rows = P(("req", "hst"), None)
    return jax.shard_map(
        functools.partial(body, n),
        mesh=mesh,
        in_specs=(rows,) * 6 + (P(("req", "hst")),),
        out_specs=(rows, rows),
        check_vma=False,
    )
```

```python
import functools
import math

import jax
import jax.numpy as jnp
from jax import lax
from jax.experimental import pallas as pl
from jax.experimental.pallas import tpu as pltpu
from jax.sharding import PartitionSpec as P

KVH = 4
DH = 128
PAIR = 2
FULL = 32767.0
TINY = 1e-30
C = math.log2(math.e) / math.sqrt(DH)
NT = (((1,), (1,)), ((), ()))
NN = (((1,), (0,)), ((), ()))


def remote(src, dst, send_sem, recv_sem, target):
    return pltpu.make_async_remote_copy(
        src_ref=src,
        dst_ref=dst,
        send_sem=send_sem,
        recv_sem=recv_sem,
        device_id={"hst": target},
        device_id_type=pl.DeviceIdType.MESH,
    )


def kernel(
    n, ctx_q, ctx_k, ctx_v, ask_q, ask_k, ask_v, valid, obuf, numr, statr,
    qbuf, kc, kvall, cnt, qraw, kraw, vraw, stage, pack, selfpack, qall, selfkv, kself, num, stat,
    count_ref,
    s_kv, s_an, s_q, s_own, s_raw,
    q_s, q_r, k_s, k_r, c_s, c_r, across_s, beside_s, near_s, far_s, a_r, f_s, r_s, n_s, n_r, t_s, t_r, go,
):
    rows = ctx_q.shape[0]
    G = ctx_q.shape[1] // (KVH * DH)
    tokens = ask_q.shape[0]
    tile = pack.shape[1]
    planes = n // KVH
    span = KVH * tile
    me = lax.axis_index("hst")
    p = me // KVH
    m = me % KVH
    is_root = me == 0
    is_last = p == planes - 1
    far = (m + 2) % KVH
    even = m % 2 == 0
    hub = (p == 0) & (m == 2)
    near = p == 1
    early = hub | (near & (m == 0))

    barrier = pltpu.get_barrier_semaphore()

    child = (me == 1) | (me == 2) | (me == KVH)

    def signal(sem, target):
        pl.semaphore_signal(
            sem, inc=1, device_id={"hst": target}, device_id_type=pl.DeviceIdType.MESH
        )

    @pl.when(child)
    def _():
        signal(barrier, 0)

    @pl.loop(1, n)
    def _(d):
        target = (me + d) % n

        @pl.when(target != 0)
        def _():
            signal(barrier, target)

    def drain(ref, sem):
        pltpu.make_async_copy(ref, ref, sem).wait()

    def cols(g):
        return pl.ds(pl.multiple_of(g * DH, DH), DH)

    raw_loads = [
        pltpu.make_async_copy(ask_q, qraw, s_raw.at[0]),
        pltpu.make_async_copy(ask_k, kraw, s_raw.at[1]),
        pltpu.make_async_copy(ask_v, vraw, s_raw.at[2]),
        pltpu.make_async_copy(valid, count_ref, s_raw.at[3]),
    ]
    for copy in raw_loads:
        copy.start()

    def load_kv(g, i, half, sem):
        src = (ctx_k, ctx_v)[i]
        return pltpu.make_async_copy(src.at[:, cols(g)], kc.at[g, i, half], sem)

    for g in range(KVH):
        for i in range(2):
            load_kv(g, i, 1, s_kv).start()

    @pl.when(is_root)
    def _():
        for g in range(KVH):
            for i in range(2):
                load_kv(g, i, 0, s_an).start()

    q_load = pltpu.make_async_copy(ctx_q, qbuf, s_q)
    q_load.start()

    own_kv = [
        pltpu.make_async_copy(ctx_k.at[:, cols(m)], kvall.at[m, 0], s_own),
        pltpu.make_async_copy(ctx_v.at[:, cols(m)], kvall.at[m, 1], s_own),
    ]
    for copy in own_kv:
        copy.start()

    for copy in raw_loads:
        copy.wait()
    for g in range(KVH):
        for h in range(G):
            at = (g * G + h) * DH
            stage[g, pl.ds(h * tokens, tokens), :] = qraw[:, at : at + DH].astype(jnp.float32)
        for i, raw in ((0, kraw), (1, vraw)):
            selfpack[g, pl.ds(i * tokens, tokens), :] = raw[:, g * DH : g * DH + DH].astype(
                jnp.float32
            )
    pack[...] = stage[...].astype(jnp.bfloat16)
    cnt[m] = jnp.full((tile, DH), count_ref[0].astype(jnp.float32)).astype(jnp.bfloat16)
    qall[me] = pack[m]

    @pl.when(is_last)
    def _():
        selfkv[me] = selfpack[m]

    drain(kc.at[:, :, 1], s_kv)
    drain(kvall.at[m], s_own)
    q_load.wait()

    def context(g):
        count = cnt[m].astype(jnp.float32)[0:1, :]
        row = lax.broadcasted_iota(jnp.int32, (rows, rows), 0)
        lane = lax.broadcasted_iota(jnp.int32, (rows, rows), 1)
        own = (lane <= row) & (lane.astype(jnp.float32) < count)
        outer = jnp.broadcast_to(me, (rows, rows)) > 0
        visible = jnp.concatenate([outer, own], axis=1)
        kept = lax.broadcasted_iota(jnp.int32, (rows, DH), 0).astype(jnp.float32) < count
        keys = kc[g, 0].reshape(2 * rows, DH)
        values = kc[g, 1].reshape(2 * rows, DH)
        at = [pl.ds(pl.multiple_of((g * G + k) * DH, DH), DH) for k in range(G)]
        s = [
            lax.dot_general(qbuf[:, x], keys, NT, preferred_element_type=jnp.float32)
            for x in at
        ]
        s = [jnp.where(visible, x, -jnp.inf) for x in s]
        top = [jnp.max(x, axis=1, keepdims=True) for x in s]
        e = [jnp.exp2((x - y) * C) for x, y in zip(s, top)]
        total = [jnp.sum(x, axis=1, keepdims=True) for x in e]
        mixed = [
            lax.dot_general(x.astype(jnp.bfloat16), values, NN, preferred_element_type=jnp.float32)
            for x in e
        ]
        for k in range(G):
            out = jnp.where(kept, mixed[k] * (1.0 / total[k]), 0.0)
            obuf[:, at[k]] = out.astype(jnp.bfloat16)

    def chunk_send(g, sem, target):
        piece = kc.at[g, :, 0]
        return remote(piece, piece, sem, a_r.at[g], target)

    def across(g):
        return chunk_send(g, across_s, p * KVH + far)

    def beside(g):
        return chunk_send(g, beside_s, p * KVH + m + 1)

    def along_near(g):
        return chunk_send(g, near_s, KVH)

    def along_far(g, q):
        return chunk_send(g, far_s, q * KVH + m)

    def head_send(g):
        if planes > 3:
            along_far(g, jnp.where(g < 2, 2, 3)).start()
        elif planes > 2:
            along_far(g, 2).start()

    def head_rest():
        if planes > 3:
            for g in (2, 3):
                along_far(g, 2).start()

    @pl.when(is_root)
    def _():
        drain(kc.at[:, :, 0], s_an)

        pl.semaphore_wait(barrier, 3)
        for g in range(KVH):
            across(g).start()
            along_near(g).start()
            beside(g).start()

        pl.semaphore_wait(go, 1)

    @pl.when(jnp.logical_not(is_root))
    def _():
        pl.semaphore_wait(barrier, n - 1)

    @pl.when(me == 1)
    def _():
        signal(go, 0)

    def q_send(target):
        return remote(pack.at[target % KVH], qall.at[me], q_s, q_r.at[p], target)

    def self_send(g):
        return remote(selfpack.at[g], selfkv.at[me], f_s, r_s, n - KVH + g)

    def cnt_send(d):
        g = (m + d) % KVH
        return remote(cnt.at[m], cnt.at[m], c_s, c_r, p * KVH + g)

    def kv_send(d):
        g = (m + d) % KVH
        return remote(kc.at[g, :, 1], kvall.at[m], k_s, k_r, p * KVH + g)

    for g in range(KVH):
        @pl.when(me != n - KVH + g)
        def _():
            q_send(n - KVH + g).start()
            self_send(g).start()

    @pl.loop(KVH, n)
    def _(i):
        target = n - 1 - i

        @pl.when(target != me)
        def _():
            q_send(target).start()

    for d in (2, 3, 1):
        cnt_send(d).start()
        kv_send(d).start()

    @pl.when(is_root)
    def _():
        for g in range(KVH):
            head_send(g)
        head_rest()

        @pl.loop(0, KVH)
        def _(g):
            context(g)

    def take(g):
        drain(kc.at[g, :, 0], a_r.at[g])

        @pl.when(hub)
        def _():
            head_send(g)

        @pl.when(even & (p < planes - 1) & ((p > 2) | ((p == 2) & (g < 2))))
        def _():
            along_far(g, p + 1).start()

        @pl.when(near & (m == 0))
        def _():
            across(g).start()

        @pl.when(even)
        def _():
            beside(g).start()

    @pl.when(early)
    def _():
        @pl.loop(0, KVH)
        def _(g):
            take(g)

    @pl.when(hub)
    def _():
        head_rest()

    drain(cnt.at[pl.ds(0, KVH - 1)], c_r)
    drain(kvall.at[pl.ds(0, KVH - 1)], k_r)

    def num_send(owner):
        return remote(num.at[owner], numr.at[me], n_s, n_r, owner)

    def stat_send(owner):
        return remote(stat.at[owner], statr.at[me], t_s, t_r, owner)

    def q_wait(q):
        @pl.when(q == p)
        def _():
            drain(qall.at[pl.ds(0, KVH - 1)], q_r.at[q])

        @pl.when(q != p)
        def _():
            drain(qall.at[pl.ds(0, KVH)], q_r.at[q])

    row = lax.broadcasted_iota(jnp.int32, (span, DH), 0)
    lane = lax.broadcasted_iota(jnp.int32, (span, DH), 1)
    diag, shifted = lane == row, lane == row + span

    def line(mask, x):
        return jnp.sum(jnp.where(mask, x, 0.0), axis=0, keepdims=True)

    def ask(with_self):
        total_rows = PAIR * span
        lane = lax.broadcasted_iota(jnp.int32, (total_rows, rows), 1).astype(jnp.float32)

        @pl.loop(0, planes // PAIR)
        def _(step):
            at_planes = [step * PAIR + k for k in range(PAIR)]
            for q in at_planes:
                q_wait(q)
            queries = jnp.concatenate(
                [qall[pl.ds(q * KVH, KVH)].reshape(span, DH) for q in at_planes], axis=0
            )
            s = [
                lax.dot_general(queries, kvall[j, 0], NT, preferred_element_type=jnp.float32)
                for j in range(KVH)
            ]
            s = [
                jnp.where(lane < cnt[j].astype(jnp.float32)[0:1, :], s[j], -jnp.inf)
                for j in range(KVH)
            ]
            values = [kvall[j, 1] for j in range(KVH)]
            top = [jnp.max(x, axis=1, keepdims=True) for x in s]
            if with_self:
                keys = kself[0].astype(jnp.bfloat16)
                s2 = lax.dot_general(queries, keys, NT, preferred_element_type=jnp.float32)
                u = lax.broadcasted_iota(jnp.int32, s2.shape, 1)
                row = lax.broadcasted_iota(jnp.int32, s2.shape, 0)
                shift = tile.bit_length() - 1
                t = ((at_planes[0] * span + row) >> shift) * tokens + (row & (tokens - 1))
                s2 = jnp.where(u <= t, s2, -jnp.inf)
                s[-1] = jnp.concatenate([s[-1], s2], axis=1)
                values[-1] = jnp.concatenate([values[-1], kself[1].astype(jnp.bfloat16)], axis=0)
                top[-1] = jnp.maximum(top[-1], jnp.max(s2, axis=1, keepdims=True))
            e = [jnp.exp2((x - y) * C) for x, y in zip(s, top)]
            part = [jnp.sum(x, axis=1, keepdims=True) for x in e]
            mixed = [
                lax.dot_general(
                    x.astype(jnp.bfloat16), v, NN, preferred_element_type=jnp.float32
                )
                for x, v in zip(e, values)
            ]
            best = functools.reduce(jnp.maximum, top)
            factor = [jnp.exp2((x - best) * C) for x in top]
            total = sum(x * y for x, y in zip(part, factor))
            summed = sum(x * y for x, y in zip(mixed, factor))
            size = jnp.maximum(jnp.max(jnp.abs(summed), axis=1, keepdims=True), TINY)
            coded = jnp.round(summed * (FULL / size)).astype(jnp.int32).astype(jnp.int16)
            for k, q in enumerate(at_planes):
                cut = slice(k * span, (k + 1) * span)
                line1 = line(diag, best[cut]) + line(shifted, total[cut])
                line2 = line(diag, size[cut])
                for j in range(KVH):
                    owner = q * KVH + j
                    at = k * span + j * tile
                    num[owner] = coded[at : at + tile]
                    stat[owner, pl.ds(0, 1)] = line1
                    stat[owner, pl.ds(1, 1)] = line2

                    @pl.when(owner != me)
                    def _():
                        num_send(owner).start()
                        stat_send(owner).start()

    @pl.when(is_last)
    def _():
        drain(selfkv.at[pl.ds(0, n - 1)], r_s)
        for source in range(n):
            for i in range(2):
                kself[i, pl.ds(source * tokens, tokens)] = selfkv[source, pl.ds(i * tokens, tokens)]
        ask(True)

    @pl.when(jnp.logical_not(is_last))
    def _():
        ask(False)

    numr[me] = num[me]
    statr[me] = stat[me]

    turn = jnp.where(p > 2, 2, 0)

    @pl.when(jnp.logical_not(early | is_root))
    def _():
        take(turn)
        take(turn + 1)

    @pl.when(jnp.logical_not(is_root))
    def _():
        @pl.loop(0, KVH)
        def _(k):
            g = (k + turn) % KVH

            @pl.when(jnp.logical_not(early) & (k > 1))
            def _():
                take(g)

            context(g)

    drain(qall.at[pl.ds(0, n - 1)], q_s)
    drain(cnt.at[pl.ds(0, KVH - 1)], c_s)
    drain(kvall.at[pl.ds(0, KVH - 1)], k_s)

    @pl.when(is_last)
    def _():
        drain(selfkv.at[pl.ds(0, KVH - 1)], f_s)

    @pl.when(jnp.logical_not(is_last))
    def _():
        drain(selfkv.at[pl.ds(0, KVH)], f_s)

    @pl.when(even)
    def _():
        drain(kc.at[:, :, 0], beside_s)

    @pl.when(is_root | (near & (m == 0)))
    def _():
        drain(kc.at[:, :, 0], across_s)

    @pl.when(is_root)
    def _():
        drain(kc.at[:, :, 0], near_s)

    if planes > 3:
        @pl.when(is_root | hub)
        def _():
            drain(kc.at[pl.ds(0, 3)], far_s)

        @pl.when(even & (p == 2))
        def _():
            drain(kc.at[pl.ds(0, 2), :, 0], far_s)

        @pl.when(even & (p > 2) & (p < planes - 1))
        def _():
            drain(kc.at[:, :, 0], far_s)
    elif planes > 2:
        @pl.when(is_root | hub)
        def _():
            drain(kc.at[:, :, 0], far_s)

    drain(num.at[pl.ds(0, n - 1)], n_s)
    drain(stat.at[pl.ds(0, n - 1)], t_s)
    drain(numr.at[pl.ds(0, n - 1)], n_r)
    drain(statr.at[pl.ds(0, n - 1)], t_r)


def finish(obuf, numr, statr, ctx_out, ask_out, fin, aout, s_out):
    n, tile, _ = numr.shape
    tokens = ask_out.shape[0]
    G = tile // tokens
    planes = n // KVH
    span = KVH * tile
    m = lax.axis_index("hst") % KVH
    ctx_copy = pltpu.make_async_copy(obuf, ctx_out, s_out.at[0])
    ctx_copy.start()
    row = lax.broadcasted_iota(jnp.int32, (span, DH), 0)
    lane = lax.broadcasted_iota(jnp.int32, (span, DH), 1)
    place = (row & (tile - 1)) + m * tile
    diag, shifted = lane == place, lane == place + span

    def column(q, k, mask):
        line = statr[pl.ds(q * KVH, KVH), pl.ds(k, 1)]
        line = jnp.broadcast_to(line, (KVH, tile, DH)).reshape(span, DH)
        return jnp.sum(jnp.where(mask, line, 0.0), axis=1, keepdims=True)

    top, part, mixed = [], [], []
    for q in range(planes):
        top.append(column(q, 0, diag))
        part.append(column(q, 0, shifted))
        coded = numr[pl.ds(q * KVH, KVH)].reshape(span, DH).astype(jnp.int32)
        mixed.append(coded.astype(jnp.float32) * (column(q, 1, diag) * (1.0 / FULL)))
    best = functools.reduce(jnp.maximum, top)
    factor = [jnp.exp2((x - best) * C) for x in top]
    total = sum(x * y for x, y in zip(part, factor))
    summed = sum(x * y for x, y in zip(mixed, factor))
    fin[...] = summed * (1.0 / total)
    for g in range(KVH):
        for h in range(G):
            at = (g * G + h) * DH
            aout[:, at : at + DH] = fin[pl.ds(g * tile + h * tokens, tokens), :].astype(jnp.bfloat16)
    ask_copy = pltpu.make_async_copy(aout, ask_out, s_out.at[1])
    ask_copy.start()
    ask_copy.wait()
    ctx_copy.wait()


def body(n, ctx_q, ctx_k, ctx_v, ask_q, ask_k, ask_v, valid):
    rows, width = ctx_q.shape
    tokens = ask_q.shape[0]
    G = width // (KVH * DH)
    tile = tokens * G
    planes = n // KVH
    dma = pltpu.SemaphoreType.DMA
    bf = jnp.bfloat16
    f32 = jnp.float32
    large = [
        pltpu.with_memory_space_constraint(x, pltpu.HBM)
        for x in (ctx_q, ctx_k, ctx_v, ask_q, ask_k, ask_v)
    ]
    hbm = pl.BlockSpec(memory_space=pltpu.HBM)
    vmem = pl.BlockSpec(memory_space=pltpu.VMEM)
    obuf, numr, statr = pl.pallas_call(
        functools.partial(kernel, n),
        out_shape=(
            jax.ShapeDtypeStruct(ctx_q.shape, bf),
            jax.ShapeDtypeStruct((n, tile, DH), jnp.int16),
            jax.ShapeDtypeStruct((n, 2, DH), f32),
        ),
        in_specs=[hbm] * 7,
        out_specs=(vmem,) * 3,
        scratch_shapes=[
            pltpu.VMEM(ctx_q.shape, bf),
            pltpu.VMEM((KVH, 2, 2, rows, DH), bf),
            pltpu.VMEM((KVH, 2, rows, DH), bf),
            pltpu.VMEM((KVH, tile, DH), bf),
            pltpu.VMEM(ask_q.shape, bf),
            pltpu.VMEM(ask_k.shape, bf),
            pltpu.VMEM(ask_v.shape, bf),
            pltpu.VMEM((KVH, tile, DH), f32),
            pltpu.VMEM((KVH, tile, DH), bf),
            pltpu.VMEM((KVH, 2 * tokens, DH), f32),
            pltpu.VMEM((n, tile, DH), bf),
            pltpu.VMEM((n, 2 * tokens, DH), f32),
            pltpu.VMEM((2, n * tokens, DH), f32),
            pltpu.VMEM((n, tile, DH), jnp.int16),
            pltpu.VMEM((n, 2, DH), f32),
            pltpu.SMEM((1,), jnp.int32),
            dma,
            dma,
            dma,
            dma,
            dma((4,)),
            dma,
            dma((planes,)),
            dma,
            dma,
            dma,
            dma,
            dma,
            dma,
            dma,
            dma,
            dma((KVH,)),
            dma,
            dma,
            dma,
            dma,
            dma,
            dma,
            pltpu.SemaphoreType.REGULAR,
        ],
        compiler_params=pltpu.CompilerParams(
            collective_id=0, has_side_effects=True, vmem_limit_bytes=16 << 20
        ),
    )(*large, valid)
    return pl.pallas_call(
        finish,
        out_shape=(
            jax.ShapeDtypeStruct(ctx_q.shape, bf),
            jax.ShapeDtypeStruct(ask_q.shape, bf),
        ),
        in_specs=[vmem] * 3,
        out_specs=(hbm, hbm),
        scratch_shapes=[
            pltpu.VMEM((KVH * tile, DH), f32),
            pltpu.VMEM(ask_q.shape, bf),
            dma((2,)),
        ],
        compiler_params=pltpu.CompilerParams(vmem_limit_bytes=8 << 20),
    )(obuf, numr, statr)


def solution(mesh):
    n = mesh.shape["hst"]
    rows = P(("req", "hst"), None)
    return jax.shard_map(
        functools.partial(body, n),
        mesh=mesh,
        in_specs=(rows,) * 6 + (P(("req", "hst")),),
        out_specs=(rows, rows),
        check_vma=False,
    )
```

```python
import functools
import math

import jax
import jax.numpy as jnp
from jax import lax
from jax.experimental import pallas as pl
from jax.experimental.pallas import tpu as pltpu
from jax.sharding import PartitionSpec as P

KVH = 4
DH = 128
PAIR = 2
FULL = 32767.0
TINY = 1e-30
C = math.log2(math.e) / math.sqrt(DH)
NT = (((1,), (1,)), ((), ()))
NN = (((1,), (0,)), ((), ()))


def remote(src, dst, send_sem, recv_sem, target):
    return pltpu.make_async_remote_copy(
        src_ref=src,
        dst_ref=dst,
        send_sem=send_sem,
        recv_sem=recv_sem,
        device_id={"hst": target},
        device_id_type=pl.DeviceIdType.MESH,
    )


def kernel(
    n, ctx_q, ctx_k, ctx_v, ask_q, ask_k, ask_v, valid, obuf, numr, statr,
    qbuf, kc, kvall, cnt, qraw, kraw, vraw, stage, pack, selfpack, qall, selfkv, kself, num, stat,
    count_ref,
    s_kv, s_an, s_q, s_own, s_raw,
    q_s, q_r, k_s, k_r, c_s, c_r, across_s, beside_s, near_s, far_s, a_r, f_s, r_s, n_s, n_r, t_s, t_r, go,
):
    rows = ctx_q.shape[0]
    G = ctx_q.shape[1] // (KVH * DH)
    tokens = ask_q.shape[0]
    tile = pack.shape[1]
    planes = n // KVH
    span = KVH * tile
    me = lax.axis_index("hst")
    p = me // KVH
    m = me % KVH
    is_root = me == 0
    is_last = p == planes - 1
    far = (m + 2) % KVH
    even = m % 2 == 0
    hub = (p == 0) & (m == 2)
    near = p == 1
    early = hub | (near & (m == 0))

    barrier = pltpu.get_barrier_semaphore()

    child = (me == 1) | (me == 2) | (me == KVH)

    def signal(sem, target):
        pl.semaphore_signal(
            sem, inc=1, device_id={"hst": target}, device_id_type=pl.DeviceIdType.MESH
        )

    @pl.when(child)
    def _():
        signal(barrier, 0)

    @pl.loop(1, n)
    def _(d):
        target = (me + d) % n

        @pl.when(target != 0)
        def _():
            signal(barrier, target)

    def drain(ref, sem):
        pltpu.make_async_copy(ref, ref, sem).wait()

    def cols(g):
        return pl.ds(pl.multiple_of(g * DH, DH), DH)

    raw_loads = [
        pltpu.make_async_copy(ask_q, qraw, s_raw.at[0]),
        pltpu.make_async_copy(ask_k, kraw, s_raw.at[1]),
        pltpu.make_async_copy(ask_v, vraw, s_raw.at[2]),
        pltpu.make_async_copy(valid, count_ref, s_raw.at[3]),
    ]
    for copy in raw_loads:
        copy.start()

    def load_kv(g, i, half, sem):
        src = (ctx_k, ctx_v)[i]
        return pltpu.make_async_copy(src.at[:, cols(g)], kc.at[g, i, half], sem)

    for g in range(KVH):
        for i in range(2):
            load_kv(g, i, 1, s_kv).start()

    @pl.when(is_root)
    def _():
        for g in range(KVH):
            for i in range(2):
                load_kv(g, i, 0, s_an).start()

    q_load = pltpu.make_async_copy(ctx_q, qbuf, s_q)
    q_load.start()

    own_kv = [
        pltpu.make_async_copy(ctx_k.at[:, cols(m)], kvall.at[m, 0], s_own),
        pltpu.make_async_copy(ctx_v.at[:, cols(m)], kvall.at[m, 1], s_own),
    ]
    for copy in own_kv:
        copy.start()

    for copy in raw_loads:
        copy.wait()
    for g in range(KVH):
        for h in range(G):
            at = (g * G + h) * DH
            stage[g, pl.ds(h * tokens, tokens), :] = qraw[:, at : at + DH].astype(jnp.float32)
        for i, raw in ((0, kraw), (1, vraw)):
            selfpack[g, pl.ds(i * tokens, tokens), :] = raw[:, g * DH : g * DH + DH].astype(
                jnp.float32
            )
    pack[...] = stage[...].astype(jnp.bfloat16)
    cnt[m] = jnp.full((tile, DH), count_ref[0].astype(jnp.float32)).astype(jnp.bfloat16)
    qall[me] = pack[m]

    @pl.when(is_last)
    def _():
        selfkv[me] = selfpack[m]

    drain(kc.at[:, :, 1], s_kv)
    drain(kvall.at[m], s_own)
    q_load.wait()

    def context(g, anchored):
        count = cnt[m].astype(jnp.float32)[0:1, :]
        row = lax.broadcasted_iota(jnp.int32, (rows, rows), 0)
        lane = lax.broadcasted_iota(jnp.int32, (rows, rows), 1)
        own = (lane <= row) & (lane.astype(jnp.float32) < count)
        kept = lax.broadcasted_iota(jnp.int32, (rows, DH), 0).astype(jnp.float32) < count
        if anchored:
            keys = kc[g, 0].reshape(2 * rows, DH)
            values = kc[g, 1].reshape(2 * rows, DH)
        else:
            keys, values = kc[g, 0, 1], kc[g, 1, 1]
        at = [pl.ds(pl.multiple_of((g * G + k) * DH, DH), DH) for k in range(G)]
        s = [
            lax.dot_general(qbuf[:, x], keys, NT, preferred_element_type=jnp.float32)
            for x in at
        ]
        if anchored:
            s = [
                jnp.concatenate(
                    [x[:, :rows], jnp.where(own, x[:, rows:], -jnp.inf)], axis=1
                )
                for x in s
            ]
        else:
            s = [jnp.where(own, x, -jnp.inf) for x in s]
        top = [jnp.max(x, axis=1, keepdims=True) for x in s]
        e = [jnp.exp2((x - y) * C) for x, y in zip(s, top)]
        total = [jnp.sum(x, axis=1, keepdims=True) for x in e]
        mixed = [
            lax.dot_general(x.astype(jnp.bfloat16), values, NN, preferred_element_type=jnp.float32)
            for x in e
        ]
        for k in range(G):
            out = jnp.where(kept, mixed[k] * (1.0 / total[k]), 0.0)
            obuf[:, at[k]] = out.astype(jnp.bfloat16)

    def chunk_send(g, sem, target):
        piece = kc.at[g, :, 0]
        return remote(piece, piece, sem, a_r.at[g], target)

    def across(g):
        return chunk_send(g, across_s, p * KVH + far)

    def beside(g):
        return chunk_send(g, beside_s, p * KVH + m + 1)

    def along_near(g):
        return chunk_send(g, near_s, KVH)

    def along_far(g, q):
        return chunk_send(g, far_s, q * KVH + m)

    def head_send(g):
        if planes > 3:
            along_far(g, jnp.where(g < 2, 2, 3)).start()
        elif planes > 2:
            along_far(g, 2).start()

    def head_rest():
        if planes > 3:
            for g in (2, 3):
                along_far(g, 2).start()

    @pl.when(is_root)
    def _():
        drain(kc.at[:, :, 0], s_an)

        pl.semaphore_wait(barrier, 3)
        for g in range(KVH):
            across(g).start()
            along_near(g).start()
            beside(g).start()

        pl.semaphore_wait(go, 1)

    @pl.when(jnp.logical_not(is_root))
    def _():
        pl.semaphore_wait(barrier, n - 1)

    @pl.when(me == 1)
    def _():
        signal(go, 0)

    def q_send(target):
        return remote(pack.at[target % KVH], qall.at[me], q_s, q_r.at[p], target)

    def self_send(g):
        return remote(selfpack.at[g], selfkv.at[me], f_s, r_s, n - KVH + g)

    mates = ((m + 2) % KVH, KVH - 1 - m, m + 1 - 2 * (m % 2))

    def cnt_send(g):
        return remote(cnt.at[m], cnt.at[m], c_s, c_r, p * KVH + g)

    def kv_send(g):
        return remote(kc.at[g, :, 1], kvall.at[m], k_s, k_r, p * KVH + g)

    for g in range(KVH):
        @pl.when(me != n - KVH + g)
        def _():
            q_send(n - KVH + g).start()
            self_send(g).start()

    @pl.when(is_last)
    def _():
        for g in mates:
            cnt_send(g).start()
            kv_send(g).start()

    @pl.loop(KVH, n)
    def _(i):
        target = jnp.where(is_last, i - KVH, n - 1 - i)

        @pl.when(target != me)
        def _():
            q_send(target).start()

    @pl.when(jnp.logical_not(is_last))
    def _():
        for g in mates:
            cnt_send(g).start()
            kv_send(g).start()

    @pl.when(is_root)
    def _():
        for g in range(KVH):
            head_send(g)
        head_rest()

        @pl.loop(0, KVH)
        def _(g):
            context(g, False)

    def take(g):
        drain(kc.at[g, :, 0], a_r.at[g])

        @pl.when(hub)
        def _():
            head_send(g)

        @pl.when(even & (p < planes - 1) & ((p > 2) | ((p == 2) & (g < 2))))
        def _():
            along_far(g, p + 1).start()

        @pl.when(near & (m == 0))
        def _():
            across(g).start()

        @pl.when(even)
        def _():
            beside(g).start()

    @pl.when(early)
    def _():
        @pl.loop(0, KVH)
        def _(g):
            take(g)

    @pl.when(hub)
    def _():
        head_rest()

    drain(cnt.at[pl.ds(0, KVH - 1)], c_r)
    drain(kvall.at[pl.ds(0, KVH - 1)], k_r)

    def num_send(owner):
        return remote(num.at[owner], numr.at[me], n_s, n_r, owner)

    def stat_send(owner):
        return remote(stat.at[owner], statr.at[me], t_s, t_r, owner)

    def q_wait(q):
        @pl.when(q == p)
        def _():
            drain(qall.at[pl.ds(0, KVH - 1)], q_r.at[q])

        @pl.when(q != p)
        def _():
            drain(qall.at[pl.ds(0, KVH)], q_r.at[q])

    row = lax.broadcasted_iota(jnp.int32, (span, DH), 0)
    lane = lax.broadcasted_iota(jnp.int32, (span, DH), 1)
    diag, shifted = lane == row, lane == row + span

    def line(mask, x):
        return jnp.sum(jnp.where(mask, x, 0.0), axis=0, keepdims=True)

    def ask(with_self):
        total_rows = PAIR * span
        lane = lax.broadcasted_iota(jnp.int32, (total_rows, rows), 1).astype(jnp.float32)

        @pl.loop(0, planes // PAIR)
        def _(step):
            at_planes = [step * PAIR + k for k in range(PAIR)]
            for q in at_planes:
                q_wait(q)
            queries = jnp.concatenate(
                [qall[pl.ds(q * KVH, KVH)].reshape(span, DH) for q in at_planes], axis=0
            )
            s = [
                lax.dot_general(queries, kvall[j, 0], NT, preferred_element_type=jnp.float32)
                for j in range(KVH)
            ]
            s = [
                jnp.where(lane < cnt[j].astype(jnp.float32)[0:1, :], s[j], -jnp.inf)
                for j in range(KVH)
            ]
            values = [kvall[j, 1] for j in range(KVH)]
            top = [jnp.max(x, axis=1, keepdims=True) for x in s]
            if with_self:
                keys = kself[0].astype(jnp.bfloat16)
                s2 = lax.dot_general(queries, keys, NT, preferred_element_type=jnp.float32)
                u = lax.broadcasted_iota(jnp.int32, s2.shape, 1)
                row = lax.broadcasted_iota(jnp.int32, s2.shape, 0)
                shift = tile.bit_length() - 1
                t = ((at_planes[0] * span + row) >> shift) * tokens + (row & (tokens - 1))
                s2 = jnp.where(u <= t, s2, -jnp.inf)
                s[-1] = jnp.concatenate([s[-1], s2], axis=1)
                values[-1] = jnp.concatenate([values[-1], kself[1].astype(jnp.bfloat16)], axis=0)
                top[-1] = jnp.maximum(top[-1], jnp.max(s2, axis=1, keepdims=True))
            e = [jnp.exp2((x - y) * C) for x, y in zip(s, top)]
            part = [jnp.sum(x, axis=1, keepdims=True) for x in e]
            mixed = [
                lax.dot_general(
                    x.astype(jnp.bfloat16), v, NN, preferred_element_type=jnp.float32
                )
                for x, v in zip(e, values)
            ]
            best = functools.reduce(jnp.maximum, top)
            factor = [jnp.exp2((x - best) * C) for x in top]
            total = sum(x * y for x, y in zip(part, factor))
            summed = sum(x * y for x, y in zip(mixed, factor))
            size = jnp.maximum(jnp.max(jnp.abs(summed), axis=1, keepdims=True), TINY)
            coded = jnp.round(summed * (FULL / size)).astype(jnp.int32).astype(jnp.int16)
            for k, q in enumerate(at_planes):
                cut = slice(k * span, (k + 1) * span)
                line1 = line(diag, best[cut]) + line(shifted, total[cut])
                line2 = line(diag, size[cut])
                for j in range(KVH):
                    owner = q * KVH + j
                    at = k * span + j * tile
                    num[owner] = coded[at : at + tile]
                    stat[owner, pl.ds(0, 1)] = line1
                    stat[owner, pl.ds(1, 1)] = line2

                    @pl.when(owner != me)
                    def _():
                        num_send(owner).start()
                        stat_send(owner).start()

    @pl.when(is_last)
    def _():
        drain(selfkv.at[pl.ds(0, n - 1)], r_s)
        for source in range(n):
            for i in range(2):
                kself[i, pl.ds(source * tokens, tokens)] = selfkv[source, pl.ds(i * tokens, tokens)]
        ask(True)

    @pl.when(jnp.logical_not(is_last))
    def _():
        ask(False)

    numr[me] = num[me]
    statr[me] = stat[me]

    turn = jnp.where(p > 2, 2, 0)

    @pl.when(jnp.logical_not(early | is_root))
    def _():
        take(turn)
        take(turn + 1)

    @pl.when(jnp.logical_not(is_root))
    def _():
        @pl.loop(0, KVH)
        def _(k):
            g = (k + turn) % KVH

            @pl.when(jnp.logical_not(early) & (k > 1))
            def _():
                take(g)

            context(g, True)

    drain(qall.at[pl.ds(0, n - 1)], q_s)
    drain(cnt.at[pl.ds(0, KVH - 1)], c_s)
    drain(kvall.at[pl.ds(0, KVH - 1)], k_s)

    @pl.when(is_last)
    def _():
        drain(selfkv.at[pl.ds(0, KVH - 1)], f_s)

    @pl.when(jnp.logical_not(is_last))
    def _():
        drain(selfkv.at[pl.ds(0, KVH)], f_s)

    @pl.when(even)
    def _():
        drain(kc.at[:, :, 0], beside_s)

    @pl.when(is_root | (near & (m == 0)))
    def _():
        drain(kc.at[:, :, 0], across_s)

    @pl.when(is_root)
    def _():
        drain(kc.at[:, :, 0], near_s)

    if planes > 3:
        @pl.when(is_root | hub)
        def _():
            drain(kc.at[pl.ds(0, 3)], far_s)

        @pl.when(even & (p == 2))
        def _():
            drain(kc.at[pl.ds(0, 2), :, 0], far_s)

        @pl.when(even & (p > 2) & (p < planes - 1))
        def _():
            drain(kc.at[:, :, 0], far_s)
    elif planes > 2:
        @pl.when(is_root | hub)
        def _():
            drain(kc.at[:, :, 0], far_s)

    drain(num.at[pl.ds(0, n - 1)], n_s)
    drain(stat.at[pl.ds(0, n - 1)], t_s)
    drain(numr.at[pl.ds(0, n - 1)], n_r)
    drain(statr.at[pl.ds(0, n - 1)], t_r)


def finish(obuf, numr, statr, ctx_out, ask_out, fin, aout, s_out):
    n, tile, _ = numr.shape
    tokens = ask_out.shape[0]
    G = tile // tokens
    planes = n // KVH
    span = KVH * tile
    m = lax.axis_index("hst") % KVH
    ctx_copy = pltpu.make_async_copy(obuf, ctx_out, s_out.at[0])
    ctx_copy.start()
    row = lax.broadcasted_iota(jnp.int32, (span, DH), 0)
    lane = lax.broadcasted_iota(jnp.int32, (span, DH), 1)
    place = (row & (tile - 1)) + m * tile
    diag, shifted = lane == place, lane == place + span

    def column(q, k, mask):
        line = statr[pl.ds(q * KVH, KVH), pl.ds(k, 1)]
        line = jnp.broadcast_to(line, (KVH, tile, DH)).reshape(span, DH)
        return jnp.sum(jnp.where(mask, line, 0.0), axis=1, keepdims=True)

    top, part, mixed = [], [], []
    for q in range(planes):
        top.append(column(q, 0, diag))
        part.append(column(q, 0, shifted))
        coded = numr[pl.ds(q * KVH, KVH)].reshape(span, DH).astype(jnp.int32)
        mixed.append(coded.astype(jnp.float32) * (column(q, 1, diag) * (1.0 / FULL)))
    best = functools.reduce(jnp.maximum, top)
    factor = [jnp.exp2((x - best) * C) for x in top]
    total = sum(x * y for x, y in zip(part, factor))
    summed = sum(x * y for x, y in zip(mixed, factor))
    fin[...] = summed * (1.0 / total)
    for g in range(KVH):
        for h in range(G):
            at = (g * G + h) * DH
            aout[:, at : at + DH] = fin[pl.ds(g * tile + h * tokens, tokens), :].astype(jnp.bfloat16)
    ask_copy = pltpu.make_async_copy(aout, ask_out, s_out.at[1])
    ask_copy.start()
    ask_copy.wait()
    ctx_copy.wait()


def body(n, ctx_q, ctx_k, ctx_v, ask_q, ask_k, ask_v, valid):
    rows, width = ctx_q.shape
    tokens = ask_q.shape[0]
    G = width // (KVH * DH)
    tile = tokens * G
    planes = n // KVH
    dma = pltpu.SemaphoreType.DMA
    bf = jnp.bfloat16
    f32 = jnp.float32
    large = [
        pltpu.with_memory_space_constraint(x, pltpu.HBM)
        for x in (ctx_q, ctx_k, ctx_v, ask_q, ask_k, ask_v)
    ]
    hbm = pl.BlockSpec(memory_space=pltpu.HBM)
    vmem = pl.BlockSpec(memory_space=pltpu.VMEM)
    obuf, numr, statr = pl.pallas_call(
        functools.partial(kernel, n),
        out_shape=(
            jax.ShapeDtypeStruct(ctx_q.shape, bf),
            jax.ShapeDtypeStruct((n, tile, DH), jnp.int16),
            jax.ShapeDtypeStruct((n, 2, DH), f32),
        ),
        in_specs=[hbm] * 7,
        out_specs=(vmem,) * 3,
        scratch_shapes=[
            pltpu.VMEM(ctx_q.shape, bf),
            pltpu.VMEM((KVH, 2, 2, rows, DH), bf),
            pltpu.VMEM((KVH, 2, rows, DH), bf),
            pltpu.VMEM((KVH, tile, DH), bf),
            pltpu.VMEM(ask_q.shape, bf),
            pltpu.VMEM(ask_k.shape, bf),
            pltpu.VMEM(ask_v.shape, bf),
            pltpu.VMEM((KVH, tile, DH), f32),
            pltpu.VMEM((KVH, tile, DH), bf),
            pltpu.VMEM((KVH, 2 * tokens, DH), f32),
            pltpu.VMEM((n, tile, DH), bf),
            pltpu.VMEM((n, 2 * tokens, DH), f32),
            pltpu.VMEM((2, n * tokens, DH), f32),
            pltpu.VMEM((n, tile, DH), jnp.int16),
            pltpu.VMEM((n, 2, DH), f32),
            pltpu.SMEM((1,), jnp.int32),
            dma,
            dma,
            dma,
            dma,
            dma((4,)),
            dma,
            dma((planes,)),
            dma,
            dma,
            dma,
            dma,
            dma,
            dma,
            dma,
            dma,
            dma((KVH,)),
            dma,
            dma,
            dma,
            dma,
            dma,
            dma,
            pltpu.SemaphoreType.REGULAR,
        ],
        compiler_params=pltpu.CompilerParams(
            collective_id=0, has_side_effects=True, vmem_limit_bytes=16 << 20
        ),
    )(*large, valid)
    return pl.pallas_call(
        finish,
        out_shape=(
            jax.ShapeDtypeStruct(ctx_q.shape, bf),
            jax.ShapeDtypeStruct(ask_q.shape, bf),
        ),
        in_specs=[vmem] * 3,
        out_specs=(hbm, hbm),
        scratch_shapes=[
            pltpu.VMEM((KVH * tile, DH), f32),
            pltpu.VMEM(ask_q.shape, bf),
            dma((2,)),
        ],
        compiler_params=pltpu.CompilerParams(vmem_limit_bytes=8 << 20),
    )(obuf, numr, statr)


def solution(mesh):
    n = mesh.shape["hst"]
    rows = P(("req", "hst"), None)
    return jax.shard_map(
        functools.partial(body, n),
        mesh=mesh,
        in_specs=(rows,) * 6 + (P(("req", "hst")),),
        out_specs=(rows, rows),
        check_vma=False,
    )
```

```python
import functools
import math

import jax
import jax.numpy as jnp
from jax import lax
from jax.experimental import pallas as pl
from jax.experimental.pallas import tpu as pltpu
from jax.sharding import PartitionSpec as P

KVH = 4
DH = 128
PAIR = 2
FULL = 32767.0
TINY = 1e-30
C = math.log2(math.e) / math.sqrt(DH)
NT = (((1,), (1,)), ((), ()))
NN = (((1,), (0,)), ((), ()))


def remote(src, dst, send_sem, recv_sem, target):
    return pltpu.make_async_remote_copy(
        src_ref=src,
        dst_ref=dst,
        send_sem=send_sem,
        recv_sem=recv_sem,
        device_id={"hst": target},
        device_id_type=pl.DeviceIdType.MESH,
    )


def kernel(
    n, ctx_q, ctx_k, ctx_v, ask_q, ask_k, ask_v, valid, obuf, numr, statr,
    qbuf, kc, kvall, cnt, qraw, kraw, vraw, stage, pack, selfpack, qall, selfkv, kself, num, stat,
    count_ref,
    s_kv, s_an, s_q, s_own, s_raw, s_cnt,
    q_s, q_r, k_s, k_r, c_s, c_r, tree_s, far_s, a_r, f_s, r_s, n_s, n_r, t_s, t_r, go,
):
    rows = ctx_q.shape[0]
    G = ctx_q.shape[1] // (KVH * DH)
    tokens = ask_q.shape[0]
    tile = pack.shape[1]
    planes = n // KVH
    span = KVH * tile
    me = lax.axis_index("hst")
    p = me // KVH
    m = me % KVH
    is_root = me == 0
    is_last = p == planes - 1
    far = (m + 2) % KVH
    even = m % 2 == 0
    hub = (p == 0) & (m == 2)
    near = p == 1
    early = hub | (near & (m == 0))

    barrier = pltpu.get_barrier_semaphore()

    child = (me == 1) | (me == 2) | (me == KVH)

    def signal(sem, target):
        pl.semaphore_signal(
            sem, inc=1, device_id={"hst": target}, device_id_type=pl.DeviceIdType.MESH
        )

    @pl.when(child)
    def _():
        signal(barrier, 0)

    @pl.loop(1, n)
    def _(d):
        target = (me + d) % n

        @pl.when(target != 0)
        def _():
            signal(barrier, target)

    def drain(ref, sem):
        pltpu.make_async_copy(ref, ref, sem).wait()

    def cols(g):
        return pl.ds(pl.multiple_of(g * DH, DH), DH)

    raw_loads = [
        pltpu.make_async_copy(ask_q, qraw, s_raw),
        pltpu.make_async_copy(ask_k, kraw, s_raw),
        pltpu.make_async_copy(ask_v, vraw, s_raw),
        pltpu.make_async_copy(valid, count_ref, s_cnt),
    ]
    for copy in raw_loads:
        copy.start()

    def load_kv(g, i, half, sem):
        src = (ctx_k, ctx_v)[i]
        return pltpu.make_async_copy(src.at[:, cols(g)], kc.at[g, i, half], sem)

    for g in range(KVH):
        for i in range(2):
            load_kv(g, i, 1, s_kv).start()

    @pl.when(is_root)
    def _():
        for g in range(KVH):
            for i in range(2):
                load_kv(g, i, 0, s_an).start()

    q_load = pltpu.make_async_copy(ctx_q, qbuf, s_q)
    q_load.start()

    own_kv = [
        pltpu.make_async_copy(ctx_k.at[:, cols(m)], kvall.at[m, 0], s_own),
        pltpu.make_async_copy(ctx_v.at[:, cols(m)], kvall.at[m, 1], s_own),
    ]
    for copy in own_kv:
        copy.start()

    drain(qall.at[pl.ds(0, KVH + 2 * KVH // G)], s_raw)
    raw_loads[-1].wait()
    for g in range(KVH):
        for h in range(G):
            at = (g * G + h) * DH
            stage[g, pl.ds(h * tokens, tokens), :] = qraw[:, at : at + DH].astype(jnp.float32)
        for i, raw in ((0, kraw), (1, vraw)):
            selfpack[g, pl.ds(i * tokens, tokens), :] = raw[:, g * DH : g * DH + DH].astype(
                jnp.float32
            )
    pack[...] = stage[...].astype(jnp.bfloat16)
    cnt[m] = jnp.full((tile, DH), count_ref[0].astype(jnp.float32)).astype(jnp.bfloat16)
    qall[me] = pack[m]

    @pl.when(is_last)
    def _():
        selfkv[me] = selfpack[m]

    drain(kc.at[:, :, 1], s_kv)
    drain(kvall.at[m], s_own)
    q_load.wait()

    def context(g, anchored):
        count = cnt[m].astype(jnp.float32)[0:1, :]
        row = lax.broadcasted_iota(jnp.int32, (rows, rows), 0)
        lane = lax.broadcasted_iota(jnp.int32, (rows, rows), 1)
        own = (lane <= row) & (lane.astype(jnp.float32) < count)
        kept = lax.broadcasted_iota(jnp.int32, (rows, DH), 0).astype(jnp.float32) < count
        if anchored:
            keys = kc[g, 0].reshape(2 * rows, DH)
            values = kc[g, 1].reshape(2 * rows, DH)
        else:
            keys, values = kc[g, 0, 1], kc[g, 1, 1]
        at = [pl.ds(pl.multiple_of((g * G + k) * DH, DH), DH) for k in range(G)]
        s = [
            lax.dot_general(qbuf[:, x], keys, NT, preferred_element_type=jnp.float32)
            for x in at
        ]
        if anchored:
            s = [
                jnp.concatenate(
                    [x[:, :rows], jnp.where(own, x[:, rows:], -jnp.inf)], axis=1
                )
                for x in s
            ]
        else:
            s = [jnp.where(own, x, -jnp.inf) for x in s]
        top = [jnp.max(x, axis=1, keepdims=True) for x in s]
        e = [jnp.exp2((x - y) * C) for x, y in zip(s, top)]
        total = [jnp.sum(x, axis=1, keepdims=True) for x in e]
        mixed = [
            lax.dot_general(x.astype(jnp.bfloat16), values, NN, preferred_element_type=jnp.float32)
            for x in e
        ]
        for k in range(G):
            out = jnp.where(kept, mixed[k] * (1.0 / total[k]), 0.0)
            obuf[:, at[k]] = out.astype(jnp.bfloat16)

    def chunk_send(g, sem, target):
        piece = kc.at[g, :, 0]
        return remote(piece, piece, sem, a_r.at[g], target)

    def across(g):
        return chunk_send(g, tree_s, p * KVH + far)

    def beside(g):
        return chunk_send(g, tree_s, p * KVH + m + 1)

    def along_near(g):
        return chunk_send(g, tree_s, KVH)

    def along_far(g, q):
        return chunk_send(g, far_s, q * KVH + m)

    def head_send(g):
        if planes > 3:
            along_far(g, jnp.where(g < 2, 2, 3)).start()
        elif planes > 2:
            along_far(g, 2).start()

    def head_rest():
        if planes > 3:
            for g in (2, 3):
                along_far(g, 2).start()

    @pl.when(is_root)
    def _():
        drain(kc.at[:, :, 0], s_an)

        pl.semaphore_wait(barrier, 3)
        for g in range(KVH):
            across(g).start()
            along_near(g).start()
            beside(g).start()

        pl.semaphore_wait(go, 1)

    @pl.when(jnp.logical_not(is_root))
    def _():
        pl.semaphore_wait(barrier, n - 1)

    @pl.when(me == 1)
    def _():
        signal(go, 0)

    def q_send(target):
        return remote(pack.at[target % KVH], qall.at[me], q_s, q_r.at[p], target)

    def self_send(g):
        return remote(selfpack.at[g], selfkv.at[me], f_s, r_s, n - KVH + g)

    mates = ((m + 2) % KVH, KVH - 1 - m, m + 1 - 2 * (m % 2))

    def cnt_send(g):
        return remote(cnt.at[m], cnt.at[m], c_s, c_r, p * KVH + g)

    def kv_send(g):
        return remote(kc.at[g, :, 1], kvall.at[m], k_s, k_r, p * KVH + g)

    for g in range(KVH):
        @pl.when(me != n - KVH + g)
        def _():
            q_send(n - KVH + g).start()
            self_send(g).start()

    @pl.when(p > 1)
    def _():
        for g in mates:
            cnt_send(g).start()
            kv_send(g).start()

    @pl.loop(KVH, n)
    def _(i):
        target = jnp.where(is_last, i - KVH, n - 1 - i)

        @pl.when(target != me)
        def _():
            q_send(target).start()

    @pl.when(p < 2)
    def _():
        for g in mates:
            cnt_send(g).start()
            kv_send(g).start()

    @pl.when(is_root)
    def _():
        for g in range(KVH):
            head_send(g)
        head_rest()

        @pl.loop(0, KVH)
        def _(g):
            context(g, False)

    def take(g):
        drain(kc.at[g, :, 0], a_r.at[g])

        @pl.when(hub)
        def _():
            head_send(g)

        @pl.when(even & (p < planes - 1) & ((p > 2) | ((p == 2) & (g < 2))))
        def _():
            along_far(g, p + 1).start()

        @pl.when(near & (m == 0))
        def _():
            across(g).start()

        @pl.when(even)
        def _():
            beside(g).start()

    @pl.when(early)
    def _():
        @pl.loop(0, KVH)
        def _(g):
            take(g)

    @pl.when(hub)
    def _():
        head_rest()

    drain(cnt.at[pl.ds(0, KVH - 1)], c_r)
    drain(kvall.at[pl.ds(0, KVH - 1)], k_r)

    def num_send(owner):
        return remote(num.at[owner], numr.at[me], n_s, n_r, owner)

    def stat_send(owner):
        return remote(stat.at[owner], statr.at[me], t_s, t_r, owner)

    def q_wait(q):
        @pl.when(q == p)
        def _():
            drain(qall.at[pl.ds(0, KVH - 1)], q_r.at[q])

        @pl.when(q != p)
        def _():
            drain(qall.at[pl.ds(0, KVH)], q_r.at[q])

    row = lax.broadcasted_iota(jnp.int32, (span, DH), 0)
    lane = lax.broadcasted_iota(jnp.int32, (span, DH), 1)
    diag, shifted = lane == row, lane == row + span

    def line(mask, x):
        return jnp.sum(jnp.where(mask, x, 0.0), axis=0, keepdims=True)

    def ask(with_self):
        total_rows = PAIR * span
        lane = lax.broadcasted_iota(jnp.int32, (total_rows, rows), 1).astype(jnp.float32)

        @pl.loop(0, planes // PAIR)
        def _(step):
            at_planes = [step * PAIR + k for k in range(PAIR)]
            for q in at_planes:
                q_wait(q)
            queries = jnp.concatenate(
                [qall[pl.ds(q * KVH, KVH)].reshape(span, DH) for q in at_planes], axis=0
            )
            s = [
                lax.dot_general(queries, kvall[j, 0], NT, preferred_element_type=jnp.float32)
                for j in range(KVH)
            ]
            s = [
                jnp.where(lane < cnt[j].astype(jnp.float32)[0:1, :], s[j], -jnp.inf)
                for j in range(KVH)
            ]
            values = [kvall[j, 1] for j in range(KVH)]
            top = [jnp.max(x, axis=1, keepdims=True) for x in s]
            if with_self:
                keys = kself[0].astype(jnp.bfloat16)
                s2 = lax.dot_general(queries, keys, NT, preferred_element_type=jnp.float32)
                u = lax.broadcasted_iota(jnp.int32, s2.shape, 1)
                row = lax.broadcasted_iota(jnp.int32, s2.shape, 0)
                shift = tile.bit_length() - 1
                t = ((at_planes[0] * span + row) >> shift) * tokens + (row & (tokens - 1))
                s2 = jnp.where(u <= t, s2, -jnp.inf)
                s[-1] = jnp.concatenate([s[-1], s2], axis=1)
                values[-1] = jnp.concatenate([values[-1], kself[1].astype(jnp.bfloat16)], axis=0)
                top[-1] = jnp.maximum(top[-1], jnp.max(s2, axis=1, keepdims=True))
            e = [jnp.exp2((x - y) * C) for x, y in zip(s, top)]
            part = [jnp.sum(x, axis=1, keepdims=True) for x in e]
            mixed = [
                lax.dot_general(
                    x.astype(jnp.bfloat16), v, NN, preferred_element_type=jnp.float32
                )
                for x, v in zip(e, values)
            ]
            best = functools.reduce(jnp.maximum, top)
            factor = [jnp.exp2((x - best) * C) for x in top]
            total = sum(x * y for x, y in zip(part, factor))
            summed = sum(x * y for x, y in zip(mixed, factor))
            size = jnp.maximum(jnp.max(jnp.abs(summed), axis=1, keepdims=True), TINY)
            coded = jnp.round(summed * (FULL / size)).astype(jnp.int32).astype(jnp.int16)
            for k, q in enumerate(at_planes):
                cut = slice(k * span, (k + 1) * span)
                line1 = line(diag, best[cut]) + line(shifted, total[cut])
                line2 = line(diag, size[cut])
                for j in range(KVH):
                    owner = q * KVH + j
                    at = k * span + j * tile
                    num[owner] = coded[at : at + tile]
                    stat[owner, pl.ds(0, 1)] = line1
                    stat[owner, pl.ds(1, 1)] = line2

                    @pl.when(owner != me)
                    def _():
                        num_send(owner).start()
                        stat_send(owner).start()

    @pl.when(is_last)
    def _():
        drain(selfkv.at[pl.ds(0, n - 1)], r_s)
        for source in range(n):
            for i in range(2):
                kself[i, pl.ds(source * tokens, tokens)] = selfkv[source, pl.ds(i * tokens, tokens)]
        ask(True)

    @pl.when(jnp.logical_not(is_last))
    def _():
        ask(False)

    numr[me] = num[me]
    statr[me] = stat[me]

    turn = jnp.where(p > 2, 2, 0)

    @pl.when(jnp.logical_not(early | is_root))
    def _():
        take(turn)
        take(turn + 1)

    @pl.when(jnp.logical_not(is_root))
    def _():
        @pl.loop(0, KVH)
        def _(k):
            g = (k + turn) % KVH

            @pl.when(jnp.logical_not(early) & (k > 1))
            def _():
                take(g)

            context(g, True)

    drain(qall.at[pl.ds(0, n - 1)], q_s)
    drain(cnt.at[pl.ds(0, KVH - 1)], c_s)
    drain(kvall.at[pl.ds(0, KVH - 1)], k_s)

    @pl.when(is_last)
    def _():
        drain(selfkv.at[pl.ds(0, KVH - 1)], f_s)

    @pl.when(jnp.logical_not(is_last))
    def _():
        drain(selfkv.at[pl.ds(0, KVH)], f_s)

    @pl.when(is_root)
    def _():
        drain(qbuf.at[:, pl.ds(0, 3 * KVH * 2 * DH)], tree_s)

    @pl.when(near & (m == 0))
    def _():
        drain(kc, tree_s)

    @pl.when(even & jnp.logical_not(is_root | (near & (m == 0))))
    def _():
        drain(kc.at[:, :, 0], tree_s)

    if planes > 3:
        @pl.when(is_root | hub)
        def _():
            drain(kc.at[pl.ds(0, 3)], far_s)

        @pl.when(even & (p == 2))
        def _():
            drain(kc.at[pl.ds(0, 2), :, 0], far_s)

        @pl.when(even & (p > 2) & (p < planes - 1))
        def _():
            drain(kc.at[:, :, 0], far_s)
    elif planes > 2:
        @pl.when(is_root | hub)
        def _():
            drain(kc.at[:, :, 0], far_s)

    drain(num.at[pl.ds(0, n - 1)], n_s)
    drain(stat.at[pl.ds(0, n - 1)], t_s)
    drain(numr.at[pl.ds(0, n - 1)], n_r)
    drain(statr.at[pl.ds(0, n - 1)], t_r)


def finish(obuf, numr, statr, ctx_out, ask_out, fin, aout, s_out):
    n, tile, _ = numr.shape
    tokens = ask_out.shape[0]
    G = tile // tokens
    planes = n // KVH
    span = KVH * tile
    m = lax.axis_index("hst") % KVH
    ctx_copy = pltpu.make_async_copy(obuf, ctx_out, s_out.at[0])
    ctx_copy.start()
    row = lax.broadcasted_iota(jnp.int32, (span, DH), 0)
    lane = lax.broadcasted_iota(jnp.int32, (span, DH), 1)
    place = (row & (tile - 1)) + m * tile
    diag, shifted = lane == place, lane == place + span

    def column(q, k, mask):
        line = statr[pl.ds(q * KVH, KVH), pl.ds(k, 1)]
        line = jnp.broadcast_to(line, (KVH, tile, DH)).reshape(span, DH)
        return jnp.sum(jnp.where(mask, line, 0.0), axis=1, keepdims=True)

    top, part, mixed = [], [], []
    for q in range(planes):
        top.append(column(q, 0, diag))
        part.append(column(q, 0, shifted))
        coded = numr[pl.ds(q * KVH, KVH)].reshape(span, DH).astype(jnp.int32)
        mixed.append(coded.astype(jnp.float32) * (column(q, 1, diag) * (1.0 / FULL)))
    best = functools.reduce(jnp.maximum, top)
    factor = [jnp.exp2((x - best) * C) for x in top]
    total = sum(x * y for x, y in zip(part, factor))
    summed = sum(x * y for x, y in zip(mixed, factor))
    fin[...] = summed * (1.0 / total)
    for g in range(KVH):
        for h in range(G):
            at = (g * G + h) * DH
            aout[:, at : at + DH] = fin[pl.ds(g * tile + h * tokens, tokens), :].astype(jnp.bfloat16)
    ask_copy = pltpu.make_async_copy(aout, ask_out, s_out.at[1])
    ask_copy.start()
    ask_copy.wait()
    ctx_copy.wait()


def body(n, ctx_q, ctx_k, ctx_v, ask_q, ask_k, ask_v, valid):
    rows, width = ctx_q.shape
    tokens = ask_q.shape[0]
    G = width // (KVH * DH)
    tile = tokens * G
    planes = n // KVH
    dma = pltpu.SemaphoreType.DMA
    bf = jnp.bfloat16
    f32 = jnp.float32
    large = [
        pltpu.with_memory_space_constraint(x, pltpu.HBM)
        for x in (ctx_q, ctx_k, ctx_v, ask_q, ask_k, ask_v)
    ]
    hbm = pl.BlockSpec(memory_space=pltpu.HBM)
    vmem = pl.BlockSpec(memory_space=pltpu.VMEM)
    obuf, numr, statr = pl.pallas_call(
        functools.partial(kernel, n),
        out_shape=(
            jax.ShapeDtypeStruct(ctx_q.shape, bf),
            jax.ShapeDtypeStruct((n, tile, DH), jnp.int16),
            jax.ShapeDtypeStruct((n, 2, DH), f32),
        ),
        in_specs=[hbm] * 7,
        out_specs=(vmem,) * 3,
        scratch_shapes=[
            pltpu.VMEM(ctx_q.shape, bf),
            pltpu.VMEM((KVH, 2, 2, rows, DH), bf),
            pltpu.VMEM((KVH, 2, rows, DH), bf),
            pltpu.VMEM((KVH, tile, DH), bf),
            pltpu.VMEM(ask_q.shape, bf),
            pltpu.VMEM(ask_k.shape, bf),
            pltpu.VMEM(ask_v.shape, bf),
            pltpu.VMEM((KVH, tile, DH), f32),
            pltpu.VMEM((KVH, tile, DH), bf),
            pltpu.VMEM((KVH, 2 * tokens, DH), f32),
            pltpu.VMEM((n, tile, DH), bf),
            pltpu.VMEM((n, 2 * tokens, DH), f32),
            pltpu.VMEM((2, n * tokens, DH), f32),
            pltpu.VMEM((n, tile, DH), jnp.int16),
            pltpu.VMEM((n, 2, DH), f32),
            pltpu.SMEM((1,), jnp.int32),
            dma,
            dma,
            dma,
            dma,
            dma,
            dma,
            dma,
            dma((planes,)),
            dma,
            dma,
            dma,
            dma,
            dma,
            dma,
            dma((KVH,)),
            dma,
            dma,
            dma,
            dma,
            dma,
            dma,
            pltpu.SemaphoreType.REGULAR,
        ],
        compiler_params=pltpu.CompilerParams(
            collective_id=0, has_side_effects=True, vmem_limit_bytes=16 << 20
        ),
    )(*large, valid)
    return pl.pallas_call(
        finish,
        out_shape=(
            jax.ShapeDtypeStruct(ctx_q.shape, bf),
            jax.ShapeDtypeStruct(ask_q.shape, bf),
        ),
        in_specs=[vmem] * 3,
        out_specs=(hbm, hbm),
        scratch_shapes=[
            pltpu.VMEM((KVH * tile, DH), f32),
            pltpu.VMEM(ask_q.shape, bf),
            dma((2,)),
        ],
        compiler_params=pltpu.CompilerParams(vmem_limit_bytes=8 << 20),
    )(obuf, numr, statr)


def solution(mesh):
    n = mesh.shape["hst"]
    rows = P(("req", "hst"), None)
    return jax.shard_map(
        functools.partial(body, n),
        mesh=mesh,
        in_specs=(rows,) * 6 + (P(("req", "hst")),),
        out_specs=(rows, rows),
        check_vma=False,
    )
```

```python
import functools
import math

import jax
import jax.numpy as jnp
from jax import lax
from jax.experimental import pallas as pl
from jax.experimental.pallas import tpu as pltpu
from jax.sharding import PartitionSpec as P

KVH = 4
DH = 128
PAIR = 2
FULL = 32767.0
TINY = 1e-30
C = math.log2(math.e) / math.sqrt(DH)
NT = (((1,), (1,)), ((), ()))
NN = (((1,), (0,)), ((), ()))


def remote(src, dst, send_sem, recv_sem, target):
    return pltpu.make_async_remote_copy(
        src_ref=src,
        dst_ref=dst,
        send_sem=send_sem,
        recv_sem=recv_sem,
        device_id={"hst": target},
        device_id_type=pl.DeviceIdType.MESH,
    )


def kernel(
    n, ctx_q, ctx_k, ctx_v, ask_q, ask_k, ask_v, valid, obuf, numr, statr,
    qbuf, kc, kvall, cnt, qraw, kraw, vraw, stage, pack, selfpack, qall, selfkv, kself, num, stat,
    count_ref,
    s_kv, s_an, s_q, s_own, s_raw, s_cnt,
    q_s, q_r, k_s, k_r, c_s, c_r, tree_s, far_s, a_r, f_s, r_s, n_s, n_r, t_s, t_r, go,
):
    rows = ctx_q.shape[0]
    G = ctx_q.shape[1] // (KVH * DH)
    tokens = ask_q.shape[0]
    tile = pack.shape[1]
    planes = n // KVH
    span = KVH * tile
    me = lax.axis_index("hst")
    p = me // KVH
    m = me % KVH
    is_root = me == 0
    is_last = p == planes - 1
    far = (m + 2) % KVH
    even = m % 2 == 0
    hub = (p == 0) & (m == 2)
    near = p == 1
    early = hub | (near & (m == 0))

    barrier = pltpu.get_barrier_semaphore()

    child = (me == 1) | (me == 2) | (me == KVH)

    def signal(sem, target):
        pl.semaphore_signal(
            sem, inc=1, device_id={"hst": target}, device_id_type=pl.DeviceIdType.MESH
        )

    @pl.when(child)
    def _():
        signal(barrier, 0)

    @pl.loop(1, n)
    def _(d):
        target = (me + d) % n

        @pl.when(target != 0)
        def _():
            signal(barrier, target)

    def drain(ref, sem):
        pltpu.make_async_copy(ref, ref, sem).wait()

    def cols(g):
        return pl.ds(pl.multiple_of(g * DH, DH), DH)

    raw_loads = [
        pltpu.make_async_copy(ask_q, qraw, s_raw),
        pltpu.make_async_copy(ask_k, kraw, s_raw),
        pltpu.make_async_copy(ask_v, vraw, s_raw),
        pltpu.make_async_copy(valid, count_ref, s_cnt),
    ]
    for copy in raw_loads:
        copy.start()

    def load_kv(g, i, half, sem):
        src = (ctx_k, ctx_v)[i]
        return pltpu.make_async_copy(src.at[:, cols(g)], kc.at[g, i, half], sem)

    for g in range(KVH):
        for i in range(2):
            load_kv(g, i, 1, s_kv).start()

    @pl.when(is_root)
    def _():
        for g in range(KVH):
            for i in range(2):
                load_kv(g, i, 0, s_an).start()

    q_load = pltpu.make_async_copy(ctx_q, qbuf, s_q)

    own_kv = [
        pltpu.make_async_copy(ctx_k.at[:, cols(m)], kvall.at[m, 0], s_own),
        pltpu.make_async_copy(ctx_v.at[:, cols(m)], kvall.at[m, 1], s_own),
    ]
    for copy in own_kv:
        copy.start()
    q_load.start()

    drain(qall.at[pl.ds(0, KVH + 2 * KVH // G)], s_raw)
    raw_loads[-1].wait()
    for g in range(KVH):
        for h in range(G):
            at = (g * G + h) * DH
            stage[g, pl.ds(h * tokens, tokens), :] = qraw[:, at : at + DH].astype(jnp.float32)
        for i, raw in ((0, kraw), (1, vraw)):
            selfpack[g, pl.ds(i * tokens, tokens), :] = raw[:, g * DH : g * DH + DH].astype(
                jnp.float32
            )
    pack[...] = stage[...].astype(jnp.bfloat16)
    cnt[m] = jnp.full((tile, DH), count_ref[0].astype(jnp.float32)).astype(jnp.bfloat16)
    qall[me] = pack[m]

    @pl.when(is_last)
    def _():
        selfkv[me] = selfpack[m]

    drain(kc.at[:, :, 1], s_kv)

    def context(g, anchored):
        count = cnt[m].astype(jnp.float32)[0:1, :]
        row = lax.broadcasted_iota(jnp.int32, (rows, rows), 0)
        lane = lax.broadcasted_iota(jnp.int32, (rows, rows), 1)
        own = (lane <= row) & (lane.astype(jnp.float32) < count)
        kept = lax.broadcasted_iota(jnp.int32, (rows, DH), 0).astype(jnp.float32) < count
        if anchored:
            keys = kc[g, 0].reshape(2 * rows, DH)
            values = kc[g, 1].reshape(2 * rows, DH)
        else:
            keys, values = kc[g, 0, 1], kc[g, 1, 1]
        at = [pl.ds(pl.multiple_of((g * G + k) * DH, DH), DH) for k in range(G)]
        s = [
            lax.dot_general(qbuf[:, x], keys, NT, preferred_element_type=jnp.float32)
            for x in at
        ]
        if anchored:
            s = [
                jnp.concatenate(
                    [x[:, :rows], jnp.where(own, x[:, rows:], -jnp.inf)], axis=1
                )
                for x in s
            ]
        else:
            s = [jnp.where(own, x, -jnp.inf) for x in s]
        top = [jnp.max(x, axis=1, keepdims=True) for x in s]
        e = [jnp.exp2((x - y) * C) for x, y in zip(s, top)]
        total = [jnp.sum(x, axis=1, keepdims=True) for x in e]
        mixed = [
            lax.dot_general(x.astype(jnp.bfloat16), values, NN, preferred_element_type=jnp.float32)
            for x in e
        ]
        for k in range(G):
            out = jnp.where(kept, mixed[k] * (1.0 / total[k]), 0.0)
            obuf[:, at[k]] = out.astype(jnp.bfloat16)

    def chunk_send(g, sem, target):
        piece = kc.at[g, :, 0]
        return remote(piece, piece, sem, a_r.at[g], target)

    def across(g):
        return chunk_send(g, tree_s, p * KVH + far)

    def beside(g):
        return chunk_send(g, tree_s, p * KVH + m + 1)

    def along_near(g):
        return chunk_send(g, tree_s, KVH)

    def along_far(g, q):
        return chunk_send(g, far_s, q * KVH + m)

    def head_send(g):
        if planes > 3:
            along_far(g, jnp.where(g < 2, 2, 3)).start()
        elif planes > 2:
            along_far(g, 2).start()

    def head_rest():
        if planes > 3:
            for g in (2, 3):
                along_far(g, 2).start()

    @pl.when(is_root)
    def _():
        drain(kc.at[:, :, 0], s_an)

        pl.semaphore_wait(barrier, 3)
        for g in range(KVH):
            across(g).start()
            along_near(g).start()
            beside(g).start()

        pl.semaphore_wait(go, 1)

    @pl.when(jnp.logical_not(is_root))
    def _():
        pl.semaphore_wait(barrier, n - 1)

    @pl.when(me == 1)
    def _():
        signal(go, 0)

    def q_send(target):
        return remote(pack.at[target % KVH], qall.at[me], q_s, q_r.at[p], target)

    def self_send(g):
        return remote(selfpack.at[g], selfkv.at[me], f_s, r_s, n - KVH + g)

    mates = ((m + 2) % KVH, KVH - 1 - m, m + 1 - 2 * (m % 2))

    def cnt_send(g):
        return remote(cnt.at[m], cnt.at[m], c_s, c_r, p * KVH + g)

    def kv_send(g):
        return remote(kc.at[g, :, 1], kvall.at[m], k_s, k_r, p * KVH + g)

    for g in range(KVH):
        @pl.when(me != n - KVH + g)
        def _():
            q_send(n - KVH + g).start()
            self_send(g).start()

    @pl.when(p > 1)
    def _():
        for g in mates:
            cnt_send(g).start()
            kv_send(g).start()

    @pl.loop(KVH, n)
    def _(i):
        target = jnp.where(is_last, i - KVH, n - 1 - i)

        @pl.when(target != me)
        def _():
            q_send(target).start()

    @pl.when(p < 2)
    def _():
        for g in mates:
            cnt_send(g).start()
            kv_send(g).start()

    drain(kvall.at[m], s_own)
    q_load.wait()

    @pl.when(is_root)
    def _():
        for g in range(KVH):
            head_send(g)
        head_rest()

        @pl.loop(0, KVH)
        def _(g):
            context(g, False)

    def take(g):
        drain(kc.at[g, :, 0], a_r.at[g])

        @pl.when(hub)
        def _():
            head_send(g)

        @pl.when(even & (p < planes - 1) & ((p > 2) | ((p == 2) & (g < 2))))
        def _():
            along_far(g, p + 1).start()

        @pl.when(near & (m == 0))
        def _():
            across(g).start()

        @pl.when(even)
        def _():
            beside(g).start()

    @pl.when(early)
    def _():
        @pl.loop(0, KVH)
        def _(g):
            take(g)

    @pl.when(hub)
    def _():
        head_rest()

    drain(cnt.at[pl.ds(0, KVH - 1)], c_r)
    drain(kvall.at[pl.ds(0, KVH - 1)], k_r)

    def num_send(owner):
        return remote(num.at[owner], numr.at[me], n_s, n_r, owner)

    def stat_send(owner):
        return remote(stat.at[owner], statr.at[me], t_s, t_r, owner)

    def q_wait(q):
        @pl.when(q == p)
        def _():
            drain(qall.at[pl.ds(0, KVH - 1)], q_r.at[q])

        @pl.when(q != p)
        def _():
            drain(qall.at[pl.ds(0, KVH)], q_r.at[q])

    row = lax.broadcasted_iota(jnp.int32, (span, DH), 0)
    lane = lax.broadcasted_iota(jnp.int32, (span, DH), 1)
    diag, shifted = lane == row, lane == row + span

    def line(mask, x):
        return jnp.sum(jnp.where(mask, x, 0.0), axis=0, keepdims=True)

    def ask(with_self):
        total_rows = PAIR * span
        lane = lax.broadcasted_iota(jnp.int32, (total_rows, rows), 1).astype(jnp.float32)

        @pl.loop(0, planes // PAIR)
        def _(step):
            at_planes = [step * PAIR + k for k in range(PAIR)]
            for q in at_planes:
                q_wait(q)
            queries = jnp.concatenate(
                [qall[pl.ds(q * KVH, KVH)].reshape(span, DH) for q in at_planes], axis=0
            )
            s = [
                lax.dot_general(queries, kvall[j, 0], NT, preferred_element_type=jnp.float32)
                for j in range(KVH)
            ]
            s = [
                jnp.where(lane < cnt[j].astype(jnp.float32)[0:1, :], s[j], -jnp.inf)
                for j in range(KVH)
            ]
            values = [kvall[j, 1] for j in range(KVH)]
            top = [jnp.max(x, axis=1, keepdims=True) for x in s]
            if with_self:
                keys = kself[0].astype(jnp.bfloat16)
                s2 = lax.dot_general(queries, keys, NT, preferred_element_type=jnp.float32)
                u = lax.broadcasted_iota(jnp.int32, s2.shape, 1)
                row = lax.broadcasted_iota(jnp.int32, s2.shape, 0)
                shift = tile.bit_length() - 1
                t = ((at_planes[0] * span + row) >> shift) * tokens + (row & (tokens - 1))
                s2 = jnp.where(u <= t, s2, -jnp.inf)
                s[-1] = jnp.concatenate([s[-1], s2], axis=1)
                values[-1] = jnp.concatenate([values[-1], kself[1].astype(jnp.bfloat16)], axis=0)
                top[-1] = jnp.maximum(top[-1], jnp.max(s2, axis=1, keepdims=True))
            e = [jnp.exp2((x - y) * C) for x, y in zip(s, top)]
            part = [jnp.sum(x, axis=1, keepdims=True) for x in e]
            mixed = [
                lax.dot_general(
                    x.astype(jnp.bfloat16), v, NN, preferred_element_type=jnp.float32
                )
                for x, v in zip(e, values)
            ]
            best = functools.reduce(jnp.maximum, top)
            factor = [jnp.exp2((x - best) * C) for x in top]
            total = sum(x * y for x, y in zip(part, factor))
            summed = sum(x * y for x, y in zip(mixed, factor))
            size = jnp.maximum(jnp.max(jnp.abs(summed), axis=1, keepdims=True), TINY)
            coded = jnp.round(summed * (FULL / size)).astype(jnp.int32).astype(jnp.int16)
            for k, q in enumerate(at_planes):
                cut = slice(k * span, (k + 1) * span)
                line1 = line(diag, best[cut]) + line(shifted, total[cut])
                line2 = line(diag, size[cut])
                for j in range(KVH):
                    owner = q * KVH + j
                    at = k * span + j * tile
                    num[owner] = coded[at : at + tile]
                    stat[owner, pl.ds(0, 1)] = line1
                    stat[owner, pl.ds(1, 1)] = line2

                    @pl.when(owner != me)
                    def _():
                        num_send(owner).start()
                        stat_send(owner).start()

    @pl.when(is_last)
    def _():
        drain(selfkv.at[pl.ds(0, n - 1)], r_s)
        for source in range(n):
            for i in range(2):
                kself[i, pl.ds(source * tokens, tokens)] = selfkv[source, pl.ds(i * tokens, tokens)]
        ask(True)

    @pl.when(jnp.logical_not(is_last))
    def _():
        ask(False)

    numr[me] = num[me]
    statr[me] = stat[me]

    turn = jnp.where(p > 2, 2, 0)

    @pl.when(jnp.logical_not(early | is_root))
    def _():
        take(turn)
        take(turn + 1)

    @pl.when(jnp.logical_not(is_root))
    def _():
        @pl.loop(0, KVH)
        def _(k):
            g = (k + turn) % KVH

            @pl.when(jnp.logical_not(early) & (k > 1))
            def _():
                take(g)

            context(g, True)

    drain(qall.at[pl.ds(0, n - 1)], q_s)
    drain(cnt.at[pl.ds(0, KVH - 1)], c_s)
    drain(kvall.at[pl.ds(0, KVH - 1)], k_s)

    @pl.when(is_last)
    def _():
        drain(selfkv.at[pl.ds(0, KVH - 1)], f_s)

    @pl.when(jnp.logical_not(is_last))
    def _():
        drain(selfkv.at[pl.ds(0, KVH)], f_s)

    @pl.when(is_root)
    def _():
        drain(qbuf.at[:, pl.ds(0, 3 * KVH * 2 * DH)], tree_s)

    @pl.when(near & (m == 0))
    def _():
        drain(kc, tree_s)

    @pl.when(even & jnp.logical_not(is_root | (near & (m == 0))))
    def _():
        drain(kc.at[:, :, 0], tree_s)

    if planes > 3:
        @pl.when(is_root | hub)
        def _():
            drain(kc.at[pl.ds(0, 3)], far_s)

        @pl.when(even & (p == 2))
        def _():
            drain(kc.at[pl.ds(0, 2), :, 0], far_s)

        @pl.when(even & (p > 2) & (p < planes - 1))
        def _():
            drain(kc.at[:, :, 0], far_s)
    elif planes > 2:
        @pl.when(is_root | hub)
        def _():
            drain(kc.at[:, :, 0], far_s)

    drain(num.at[pl.ds(0, n - 1)], n_s)
    drain(stat.at[pl.ds(0, n - 1)], t_s)
    drain(numr.at[pl.ds(0, n - 1)], n_r)
    drain(statr.at[pl.ds(0, n - 1)], t_r)


def finish(obuf, numr, statr, ctx_out, ask_out, fin, aout, s_out):
    n, tile, _ = numr.shape
    tokens = ask_out.shape[0]
    G = tile // tokens
    planes = n // KVH
    span = KVH * tile
    m = lax.axis_index("hst") % KVH
    ctx_copy = pltpu.make_async_copy(obuf, ctx_out, s_out.at[0])
    ctx_copy.start()
    row = lax.broadcasted_iota(jnp.int32, (span, DH), 0)
    lane = lax.broadcasted_iota(jnp.int32, (span, DH), 1)
    place = (row & (tile - 1)) + m * tile
    diag, shifted = lane == place, lane == place + span

    def column(q, k, mask):
        line = statr[pl.ds(q * KVH, KVH), pl.ds(k, 1)]
        line = jnp.broadcast_to(line, (KVH, tile, DH)).reshape(span, DH)
        return jnp.sum(jnp.where(mask, line, 0.0), axis=1, keepdims=True)

    top, part, mixed = [], [], []
    for q in range(planes):
        top.append(column(q, 0, diag))
        part.append(column(q, 0, shifted))
        coded = numr[pl.ds(q * KVH, KVH)].reshape(span, DH).astype(jnp.int32)
        mixed.append(coded.astype(jnp.float32) * (column(q, 1, diag) * (1.0 / FULL)))
    best = functools.reduce(jnp.maximum, top)
    factor = [jnp.exp2((x - best) * C) for x in top]
    total = sum(x * y for x, y in zip(part, factor))
    summed = sum(x * y for x, y in zip(mixed, factor))
    fin[...] = summed * (1.0 / total)
    for g in range(KVH):
        for h in range(G):
            at = (g * G + h) * DH
            aout[:, at : at + DH] = fin[pl.ds(g * tile + h * tokens, tokens), :].astype(jnp.bfloat16)
    ask_copy = pltpu.make_async_copy(aout, ask_out, s_out.at[1])
    ask_copy.start()
    ask_copy.wait()
    ctx_copy.wait()


def body(n, ctx_q, ctx_k, ctx_v, ask_q, ask_k, ask_v, valid):
    rows, width = ctx_q.shape
    tokens = ask_q.shape[0]
    G = width // (KVH * DH)
    tile = tokens * G
    planes = n // KVH
    dma = pltpu.SemaphoreType.DMA
    bf = jnp.bfloat16
    f32 = jnp.float32
    large = [
        pltpu.with_memory_space_constraint(x, pltpu.HBM)
        for x in (ctx_q, ctx_k, ctx_v, ask_q, ask_k, ask_v)
    ]
    hbm = pl.BlockSpec(memory_space=pltpu.HBM)
    vmem = pl.BlockSpec(memory_space=pltpu.VMEM)
    obuf, numr, statr = pl.pallas_call(
        functools.partial(kernel, n),
        out_shape=(
            jax.ShapeDtypeStruct(ctx_q.shape, bf),
            jax.ShapeDtypeStruct((n, tile, DH), jnp.int16),
            jax.ShapeDtypeStruct((n, 2, DH), f32),
        ),
        in_specs=[hbm] * 7,
        out_specs=(vmem,) * 3,
        scratch_shapes=[
            pltpu.VMEM(ctx_q.shape, bf),
            pltpu.VMEM((KVH, 2, 2, rows, DH), bf),
            pltpu.VMEM((KVH, 2, rows, DH), bf),
            pltpu.VMEM((KVH, tile, DH), bf),
            pltpu.VMEM(ask_q.shape, bf),
            pltpu.VMEM(ask_k.shape, bf),
            pltpu.VMEM(ask_v.shape, bf),
            pltpu.VMEM((KVH, tile, DH), f32),
            pltpu.VMEM((KVH, tile, DH), bf),
            pltpu.VMEM((KVH, 2 * tokens, DH), f32),
            pltpu.VMEM((n, tile, DH), bf),
            pltpu.VMEM((n, 2 * tokens, DH), f32),
            pltpu.VMEM((2, n * tokens, DH), f32),
            pltpu.VMEM((n, tile, DH), jnp.int16),
            pltpu.VMEM((n, 2, DH), f32),
            pltpu.SMEM((1,), jnp.int32),
            dma,
            dma,
            dma,
            dma,
            dma,
            dma,
            dma,
            dma((planes,)),
            dma,
            dma,
            dma,
            dma,
            dma,
            dma,
            dma((KVH,)),
            dma,
            dma,
            dma,
            dma,
            dma,
            dma,
            pltpu.SemaphoreType.REGULAR,
        ],
        compiler_params=pltpu.CompilerParams(
            collective_id=0, has_side_effects=True, vmem_limit_bytes=16 << 20
        ),
    )(*large, valid)
    return pl.pallas_call(
        finish,
        out_shape=(
            jax.ShapeDtypeStruct(ctx_q.shape, bf),
            jax.ShapeDtypeStruct(ask_q.shape, bf),
        ),
        in_specs=[vmem] * 3,
        out_specs=(hbm, hbm),
        scratch_shapes=[
            pltpu.VMEM((KVH * tile, DH), f32),
            pltpu.VMEM(ask_q.shape, bf),
            dma((2,)),
        ],
        compiler_params=pltpu.CompilerParams(vmem_limit_bytes=8 << 20),
    )(obuf, numr, statr)


def solution(mesh):
    n = mesh.shape["hst"]
    rows = P(("req", "hst"), None)
    return jax.shard_map(
        functools.partial(body, n),
        mesh=mesh,
        in_specs=(rows,) * 6 + (P(("req", "hst")),),
        out_specs=(rows, rows),
        check_vma=False,
    )
```

```python
import functools
import math

import jax
import jax.numpy as jnp
from jax import lax
from jax.experimental import pallas as pl
from jax.experimental.pallas import tpu as pltpu
from jax.sharding import PartitionSpec as P

KVH = 4
DH = 128
PAIR = 2
FULL = 32767.0
TINY = 1e-30
C = math.log2(math.e) / math.sqrt(DH)
NT = (((1,), (1,)), ((), ()))
NN = (((1,), (0,)), ((), ()))


def remote(src, dst, send_sem, recv_sem, target):
    return pltpu.make_async_remote_copy(
        src_ref=src,
        dst_ref=dst,
        send_sem=send_sem,
        recv_sem=recv_sem,
        device_id={"hst": target},
        device_id_type=pl.DeviceIdType.MESH,
    )


def kernel(
    n, ctx_q, ctx_k, ctx_v, ask_q, ask_k, ask_v, valid, obuf, numr, statr,
    qbuf, kc, kvall, cnt, qraw, kraw, vraw, stage, pack, selfpack, qall, selfkv, kself, num, stat,
    s_kv, s_an, s_q, s_own, s_raw,
    q_s, q_r, k_s, k_r, c_s, c_r, tree_s, far_s, a_r, f_s, r_s, n_s, n_r, t_s, t_r, go,
):
    rows = ctx_q.shape[0]
    G = ctx_q.shape[1] // (KVH * DH)
    tokens = ask_q.shape[0]
    tile = pack.shape[1]
    planes = n // KVH
    span = KVH * tile
    me = lax.axis_index("hst")
    p = me // KVH
    m = me % KVH
    is_root = me == 0
    is_last = p == planes - 1
    far = (m + 2) % KVH
    even = m % 2 == 0
    hub = (p == 0) & (m == 2)
    near = p == 1
    early = hub | (near & (m == 0))

    barrier = pltpu.get_barrier_semaphore()

    child = (me == 1) | (me == 2) | (me == KVH)

    def signal(sem, target):
        pl.semaphore_signal(
            sem, inc=1, device_id={"hst": target}, device_id_type=pl.DeviceIdType.MESH
        )

    @pl.when(child)
    def _():
        signal(barrier, 0)

    @pl.loop(1, n)
    def _(d):
        target = (me + d) % n

        @pl.when(target != 0)
        def _():
            signal(barrier, target)

    def drain(ref, sem):
        pltpu.make_async_copy(ref, ref, sem).wait()

    def cols(g):
        return pl.ds(pl.multiple_of(g * DH, DH), DH)

    raw_loads = [
        pltpu.make_async_copy(ask_q, qraw, s_raw),
        pltpu.make_async_copy(ask_k, kraw, s_raw),
        pltpu.make_async_copy(ask_v, vraw, s_raw),
    ]
    for copy in raw_loads:
        copy.start()

    def load_kv(g, i, half, sem):
        src = (ctx_k, ctx_v)[i]
        return pltpu.make_async_copy(src.at[:, cols(g)], kc.at[g, i, half], sem)

    for g in range(KVH):
        for i in range(2):
            load_kv(g, i, 1, s_kv).start()

    @pl.when(is_root)
    def _():
        for g in range(KVH):
            for i in range(2):
                load_kv(g, i, 0, s_an).start()

    q_load = pltpu.make_async_copy(ctx_q, qbuf, s_q)

    own_kv = [
        pltpu.make_async_copy(ctx_k.at[:, cols(m)], kvall.at[m, 0], s_own),
        pltpu.make_async_copy(ctx_v.at[:, cols(m)], kvall.at[m, 1], s_own),
    ]
    for copy in own_kv:
        copy.start()
    q_load.start()

    drain(qall.at[pl.ds(0, KVH + 2 * KVH // G)], s_raw)
    for g in range(KVH):
        for h in range(G):
            at = (g * G + h) * DH
            stage[g, pl.ds(h * tokens, tokens), :] = qraw[:, at : at + DH].astype(jnp.float32)
        for i, raw in ((0, kraw), (1, vraw)):
            selfpack[g, pl.ds(i * tokens, tokens), :] = raw[:, g * DH : g * DH + DH].astype(
                jnp.float32
            )
    pack[...] = stage[...].astype(jnp.bfloat16)
    cnt[m] = jnp.full((tile, DH), valid[0].astype(jnp.float32)).astype(jnp.bfloat16)
    qall[me] = pack[m]

    @pl.when(is_last)
    def _():
        selfkv[me] = selfpack[m]

    drain(kc.at[:, :, 1], s_kv)

    def context(g, anchored):
        count = cnt[m].astype(jnp.float32)[0:1, :]
        row = lax.broadcasted_iota(jnp.int32, (rows, rows), 0)
        lane = lax.broadcasted_iota(jnp.int32, (rows, rows), 1)
        own = (lane <= row) & (lane.astype(jnp.float32) < count)
        kept = lax.broadcasted_iota(jnp.int32, (rows, DH), 0).astype(jnp.float32) < count
        if anchored:
            keys = kc[g, 0].reshape(2 * rows, DH)
            values = kc[g, 1].reshape(2 * rows, DH)
        else:
            keys, values = kc[g, 0, 1], kc[g, 1, 1]
        at = [pl.ds(pl.multiple_of((g * G + k) * DH, DH), DH) for k in range(G)]
        s = [
            lax.dot_general(qbuf[:, x], keys, NT, preferred_element_type=jnp.float32)
            for x in at
        ]
        if anchored:
            s = [
                jnp.concatenate(
                    [x[:, :rows], jnp.where(own, x[:, rows:], -jnp.inf)], axis=1
                )
                for x in s
            ]
        else:
            s = [jnp.where(own, x, -jnp.inf) for x in s]
        top = [jnp.max(x, axis=1, keepdims=True) for x in s]
        e = [jnp.exp2((x - y) * C) for x, y in zip(s, top)]
        total = [jnp.sum(x, axis=1, keepdims=True) for x in e]
        mixed = [
            lax.dot_general(x.astype(jnp.bfloat16), values, NN, preferred_element_type=jnp.float32)
            for x in e
        ]
        for k in range(G):
            out = jnp.where(kept, mixed[k] * (1.0 / total[k]), 0.0)
            obuf[:, at[k]] = out.astype(jnp.bfloat16)

    def chunk_send(g, sem, target):
        piece = kc.at[g, :, 0]
        return remote(piece, piece, sem, a_r.at[g], target)

    def across(g):
        return chunk_send(g, tree_s, p * KVH + far)

    def beside(g):
        return chunk_send(g, tree_s, p * KVH + m + 1)

    def along_near(g):
        return chunk_send(g, tree_s, KVH)

    def along_far(g, q):
        return chunk_send(g, far_s, q * KVH + m)

    def head_send(g):
        if planes > 3:
            along_far(g, jnp.where(g < 2, 2, 3)).start()
        elif planes > 2:
            along_far(g, 2).start()

    def head_rest():
        if planes > 3:
            for g in (2, 3):
                along_far(g, 2).start()

    @pl.when(is_root)
    def _():
        drain(kc.at[:, :, 0], s_an)

        pl.semaphore_wait(barrier, 3)
        for g in range(KVH):
            across(g).start()
            along_near(g).start()
            beside(g).start()

        pl.semaphore_wait(go, 1)

    @pl.when(jnp.logical_not(is_root))
    def _():
        pl.semaphore_wait(barrier, n - 1)

    @pl.when(me == 1)
    def _():
        signal(go, 0)

    def q_send(target):
        return remote(pack.at[target % KVH], qall.at[me], q_s, q_r.at[p], target)

    def self_send(g):
        return remote(selfpack.at[g], selfkv.at[me], f_s, r_s, n - KVH + g)

    mates = ((m + 2) % KVH, KVH - 1 - m, m + 1 - 2 * (m % 2))

    def cnt_send(g):
        return remote(cnt.at[m], cnt.at[m], c_s, c_r, p * KVH + g)

    def kv_send(g):
        return remote(kc.at[g, :, 1], kvall.at[m], k_s, k_r, p * KVH + g)

    for g in range(KVH):
        @pl.when(me != n - KVH + g)
        def _():
            q_send(n - KVH + g).start()
            self_send(g).start()

    @pl.when(p > 1)
    def _():
        for g in mates:
            cnt_send(g).start()
            kv_send(g).start()

    @pl.loop(KVH, n)
    def _(i):
        target = jnp.where(is_last, i - KVH, n - 1 - i)

        @pl.when(target != me)
        def _():
            q_send(target).start()

    @pl.when(p < 2)
    def _():
        for g in mates:
            cnt_send(g).start()
            kv_send(g).start()

    drain(kvall.at[m], s_own)
    q_load.wait()

    @pl.when(is_root)
    def _():
        for g in range(KVH):
            head_send(g)
        head_rest()

        @pl.loop(0, KVH)
        def _(g):
            context(g, False)

    def take(g):
        drain(kc.at[g, :, 0], a_r.at[g])

        @pl.when(hub)
        def _():
            head_send(g)

        @pl.when(even & (p < planes - 1) & ((p > 2) | ((p == 2) & (g < 2))))
        def _():
            along_far(g, p + 1).start()

        @pl.when(near & (m == 0))
        def _():
            across(g).start()

        @pl.when(even)
        def _():
            beside(g).start()

    @pl.when(early)
    def _():
        @pl.loop(0, KVH)
        def _(g):
            take(g)

    @pl.when(hub)
    def _():
        head_rest()

    drain(cnt.at[pl.ds(0, KVH - 1)], c_r)
    drain(kvall.at[pl.ds(0, KVH - 1)], k_r)

    def num_send(owner):
        return remote(num.at[owner], numr.at[me], n_s, n_r, owner)

    def stat_send(owner):
        return remote(stat.at[owner], statr.at[me], t_s, t_r, owner)

    def q_wait(q):
        @pl.when(q == p)
        def _():
            drain(qall.at[pl.ds(0, KVH - 1)], q_r.at[q])

        @pl.when(q != p)
        def _():
            drain(qall.at[pl.ds(0, KVH)], q_r.at[q])

    row = lax.broadcasted_iota(jnp.int32, (span, DH), 0)
    lane = lax.broadcasted_iota(jnp.int32, (span, DH), 1)
    diag, shifted = lane == row, lane == row + span

    def line(mask, x):
        return jnp.sum(jnp.where(mask, x, 0.0), axis=0, keepdims=True)

    def ask(with_self):
        total_rows = PAIR * span
        lane = lax.broadcasted_iota(jnp.int32, (total_rows, rows), 1).astype(jnp.float32)

        @pl.loop(0, planes // PAIR)
        def _(step):
            at_planes = [step * PAIR + k for k in range(PAIR)]
            for q in at_planes:
                q_wait(q)
            queries = jnp.concatenate(
                [qall[pl.ds(q * KVH, KVH)].reshape(span, DH) for q in at_planes], axis=0
            )
            s = [
                lax.dot_general(queries, kvall[j, 0], NT, preferred_element_type=jnp.float32)
                for j in range(KVH)
            ]
            s = [
                jnp.where(lane < cnt[j].astype(jnp.float32)[0:1, :], s[j], -jnp.inf)
                for j in range(KVH)
            ]
            values = [kvall[j, 1] for j in range(KVH)]
            top = [jnp.max(x, axis=1, keepdims=True) for x in s]
            if with_self:
                keys = kself[0].astype(jnp.bfloat16)
                s2 = lax.dot_general(queries, keys, NT, preferred_element_type=jnp.float32)
                u = lax.broadcasted_iota(jnp.int32, s2.shape, 1)
                row = lax.broadcasted_iota(jnp.int32, s2.shape, 0)
                shift = tile.bit_length() - 1
                t = ((at_planes[0] * span + row) >> shift) * tokens + (row & (tokens - 1))
                s2 = jnp.where(u <= t, s2, -jnp.inf)
                s[-1] = jnp.concatenate([s[-1], s2], axis=1)
                values[-1] = jnp.concatenate([values[-1], kself[1].astype(jnp.bfloat16)], axis=0)
                top[-1] = jnp.maximum(top[-1], jnp.max(s2, axis=1, keepdims=True))
            e = [jnp.exp2((x - y) * C) for x, y in zip(s, top)]
            part = [jnp.sum(x, axis=1, keepdims=True) for x in e]
            mixed = [
                lax.dot_general(
                    x.astype(jnp.bfloat16), v, NN, preferred_element_type=jnp.float32
                )
                for x, v in zip(e, values)
            ]
            best = functools.reduce(jnp.maximum, top)
            factor = [jnp.exp2((x - best) * C) for x in top]
            total = sum(x * y for x, y in zip(part, factor))
            summed = sum(x * y for x, y in zip(mixed, factor))
            size = jnp.maximum(jnp.max(jnp.abs(summed), axis=1, keepdims=True), TINY)
            coded = jnp.round(summed * (FULL / size)).astype(jnp.int32).astype(jnp.int16)
            for k, q in enumerate(at_planes):
                cut = slice(k * span, (k + 1) * span)
                line1 = line(diag, best[cut]) + line(shifted, total[cut])
                line2 = line(diag, size[cut])
                for j in range(KVH):
                    owner = q * KVH + j
                    at = k * span + j * tile
                    num[owner] = coded[at : at + tile]
                    stat[owner, pl.ds(0, 1)] = line1
                    stat[owner, pl.ds(1, 1)] = line2

                    @pl.when(owner != me)
                    def _():
                        num_send(owner).start()
                        stat_send(owner).start()

    @pl.when(is_last)
    def _():
        drain(selfkv.at[pl.ds(0, n - 1)], r_s)
        for source in range(n):
            for i in range(2):
                kself[i, pl.ds(source * tokens, tokens)] = selfkv[source, pl.ds(i * tokens, tokens)]
        ask(True)

    @pl.when(jnp.logical_not(is_last))
    def _():
        ask(False)

    numr[me] = num[me]
    statr[me] = stat[me]

    turn = jnp.where(p > 2, 2, 0)

    @pl.when(jnp.logical_not(early | is_root))
    def _():
        take(turn)
        take(turn + 1)

    @pl.when(jnp.logical_not(is_root))
    def _():
        @pl.loop(0, KVH)
        def _(k):
            g = (k + turn) % KVH

            @pl.when(jnp.logical_not(early) & (k > 1))
            def _():
                take(g)

            context(g, True)

    drain(qall.at[pl.ds(0, n - 1)], q_s)
    drain(cnt.at[pl.ds(0, KVH - 1)], c_s)
    drain(kvall.at[pl.ds(0, KVH - 1)], k_s)

    @pl.when(is_last)
    def _():
        drain(selfkv.at[pl.ds(0, KVH - 1)], f_s)

    @pl.when(jnp.logical_not(is_last))
    def _():
        drain(selfkv.at[pl.ds(0, KVH)], f_s)

    @pl.when(is_root)
    def _():
        drain(qbuf.at[:, pl.ds(0, 3 * KVH * 2 * DH)], tree_s)

    @pl.when(near & (m == 0))
    def _():
        drain(kc, tree_s)

    @pl.when(even & jnp.logical_not(is_root | (near & (m == 0))))
    def _():
        drain(kc.at[:, :, 0], tree_s)

    if planes > 3:
        @pl.when(is_root | hub)
        def _():
            drain(kc.at[pl.ds(0, 3)], far_s)

        @pl.when(even & (p == 2))
        def _():
            drain(kc.at[pl.ds(0, 2), :, 0], far_s)

        @pl.when(even & (p > 2) & (p < planes - 1))
        def _():
            drain(kc.at[:, :, 0], far_s)
    elif planes > 2:
        @pl.when(is_root | hub)
        def _():
            drain(kc.at[:, :, 0], far_s)

    drain(num.at[pl.ds(0, n - 1)], n_s)
    drain(stat.at[pl.ds(0, n - 1)], t_s)
    drain(numr.at[pl.ds(0, n - 1)], n_r)
    drain(statr.at[pl.ds(0, n - 1)], t_r)


def finish(obuf, numr, statr, ctx_out, ask_out, fin, aout, s_out):
    n, tile, _ = numr.shape
    tokens = ask_out.shape[0]
    G = tile // tokens
    planes = n // KVH
    span = KVH * tile
    m = lax.axis_index("hst") % KVH
    ctx_copy = pltpu.make_async_copy(obuf, ctx_out, s_out.at[0])
    ctx_copy.start()
    row = lax.broadcasted_iota(jnp.int32, (span, DH), 0)
    lane = lax.broadcasted_iota(jnp.int32, (span, DH), 1)
    place = (row & (tile - 1)) + m * tile
    diag, shifted = lane == place, lane == place + span

    def column(q, k, mask):
        line = statr[pl.ds(q * KVH, KVH), pl.ds(k, 1)]
        line = jnp.broadcast_to(line, (KVH, tile, DH)).reshape(span, DH)
        return jnp.sum(jnp.where(mask, line, 0.0), axis=1, keepdims=True)

    top, part, mixed = [], [], []
    for q in range(planes):
        top.append(column(q, 0, diag))
        part.append(column(q, 0, shifted))
        coded = numr[pl.ds(q * KVH, KVH)].reshape(span, DH).astype(jnp.int32)
        mixed.append(coded.astype(jnp.float32) * (column(q, 1, diag) * (1.0 / FULL)))
    best = functools.reduce(jnp.maximum, top)
    factor = [jnp.exp2((x - best) * C) for x in top]
    total = sum(x * y for x, y in zip(part, factor))
    summed = sum(x * y for x, y in zip(mixed, factor))
    fin[...] = summed * (1.0 / total)
    for g in range(KVH):
        for h in range(G):
            at = (g * G + h) * DH
            aout[:, at : at + DH] = fin[pl.ds(g * tile + h * tokens, tokens), :].astype(jnp.bfloat16)
    ask_copy = pltpu.make_async_copy(aout, ask_out, s_out.at[1])
    ask_copy.start()
    ask_copy.wait()
    ctx_copy.wait()


def body(n, ctx_q, ctx_k, ctx_v, ask_q, ask_k, ask_v, valid):
    rows, width = ctx_q.shape
    tokens = ask_q.shape[0]
    G = width // (KVH * DH)
    tile = tokens * G
    planes = n // KVH
    dma = pltpu.SemaphoreType.DMA
    bf = jnp.bfloat16
    f32 = jnp.float32
    large = [
        pltpu.with_memory_space_constraint(x, pltpu.HBM)
        for x in (ctx_q, ctx_k, ctx_v, ask_q, ask_k, ask_v)
    ]
    hbm = pl.BlockSpec(memory_space=pltpu.HBM)
    vmem = pl.BlockSpec(memory_space=pltpu.VMEM)
    obuf, numr, statr = pl.pallas_call(
        functools.partial(kernel, n),
        out_shape=(
            jax.ShapeDtypeStruct(ctx_q.shape, bf),
            jax.ShapeDtypeStruct((n, tile, DH), jnp.int16),
            jax.ShapeDtypeStruct((n, 2, DH), f32),
        ),
        in_specs=[hbm] * 6 + [pl.BlockSpec(memory_space=pltpu.SMEM)],
        out_specs=(vmem,) * 3,
        scratch_shapes=[
            pltpu.VMEM(ctx_q.shape, bf),
            pltpu.VMEM((KVH, 2, 2, rows, DH), bf),
            pltpu.VMEM((KVH, 2, rows, DH), bf),
            pltpu.VMEM((KVH, tile, DH), bf),
            pltpu.VMEM(ask_q.shape, bf),
            pltpu.VMEM(ask_k.shape, bf),
            pltpu.VMEM(ask_v.shape, bf),
            pltpu.VMEM((KVH, tile, DH), f32),
            pltpu.VMEM((KVH, tile, DH), bf),
            pltpu.VMEM((KVH, 2 * tokens, DH), f32),
            pltpu.VMEM((n, tile, DH), bf),
            pltpu.VMEM((n, 2 * tokens, DH), f32),
            pltpu.VMEM((2, n * tokens, DH), f32),
            pltpu.VMEM((n, tile, DH), jnp.int16),
            pltpu.VMEM((n, 2, DH), f32),
            dma,
            dma,
            dma,
            dma,
            dma,
            dma,
            dma((planes,)),
            dma,
            dma,
            dma,
            dma,
            dma,
            dma,
            dma((KVH,)),
            dma,
            dma,
            dma,
            dma,
            dma,
            dma,
            pltpu.SemaphoreType.REGULAR,
        ],
        compiler_params=pltpu.CompilerParams(
            collective_id=0, has_side_effects=True, vmem_limit_bytes=16 << 20
        ),
    )(*large, valid)
    return pl.pallas_call(
        finish,
        out_shape=(
            jax.ShapeDtypeStruct(ctx_q.shape, bf),
            jax.ShapeDtypeStruct(ask_q.shape, bf),
        ),
        in_specs=[vmem] * 3,
        out_specs=(hbm, hbm),
        scratch_shapes=[
            pltpu.VMEM((KVH * tile, DH), f32),
            pltpu.VMEM(ask_q.shape, bf),
            dma((2,)),
        ],
        compiler_params=pltpu.CompilerParams(vmem_limit_bytes=8 << 20),
    )(obuf, numr, statr)


def solution(mesh):
    n = mesh.shape["hst"]
    rows = P(("req", "hst"), None)
    return jax.shard_map(
        functools.partial(body, n),
        mesh=mesh,
        in_specs=(rows,) * 6 + (P(("req", "hst")),),
        out_specs=(rows, rows),
        check_vma=False,
    )
```
